32 devices in a mesh: section: 4 (over x, core), dp: 8 (over z, y).
Axes of the slice: x: 2, y: 2, z: 4, core: 2. Of those that a mesh axis runs over, the one named last changes fastest.
Arguments:
- inputs: bfloat16 [8, 128, 8192], P(None, 'dp', 'section'), may hold values from -50 to 50
- cotangent: bfloat16 [8, 128, 8192], P(None, 'dp', 'section'), may hold values from -0.29882812 to 0.29882812
- first_factor: bfloat16 [4, 64, 128, 128], P('section'), may hold values from -0.5 to 0.5
- second_factor: bfloat16 [4, 64, 128, 128], P('section'), may hold values from -0.5 to 0.5
- gains: float32 [4, 8192], P('section'), may hold values from 0.1 to 1.9
- mixing: int32 [4, 8192], P('section'), may hold values from 0 to 8191, as said below
- order: int32 [8], replicated, may hold values from 0 to 7, each once
Outputs:
- first_grads: bfloat16 [4, 64, 128, 128], P('section')
- second_grads: bfloat16 [4, 64, 128, 128], P('section')
The draws below stay inside these ranges and needn't reach their ends.
Inputs may be any that keep to these rules, and one draw needn't show every extreme that they name: Each row l is a stride permutation with permuted blocks and lanes: mixing[l, a*64+e] = pb[e]*128 + pa[a] for a < 128, e < 64, where pb is a permutation of 0 to 63 and pa one of 0 to 127, both drawn afresh for each layer. `order`: a permutation of 0 to 7.
All inputs are finite; a program needn't handle non-finite values.
Results may differ from the reference program's by a relative error of at most 0.015.
Values may be sent and summed in bfloat16 or wider, within the bound.
A program may use at most 64 MiB of HBM per device.

```python
import math
import jax
import jax.numpy as jnp
from jax import lax

D = 8192
BLOCK = 128
NBLK = 64
LAYERS = 4
MICRO = 8
TOK_MB = 16
TOKENS = 128
N_DP = 8


def draw_inputs(key, part):
    keys = jax.random.split(jax.random.fold_in(key, 11), 2)
    row_scale = jnp.exp(jax.random.uniform(keys[1], (MICRO, TOKENS, 1), jnp.float32) * math.log(10.0))
    base = jnp.clip(jax.random.normal(keys[0], (MICRO, TOKENS, D), jnp.float32), -5.0, 5.0)
    return (base * row_scale).astype(jnp.bfloat16)


def mixing_row_draw(layer_key):
    keys = jax.random.split(layer_key, 2)
    block_perm = jax.random.permutation(keys[0], NBLK).astype(jnp.int32)
    lane_perm = jax.random.permutation(keys[1], BLOCK).astype(jnp.int32)
    return (block_perm[None, :] * BLOCK + lane_perm[:, None]).reshape(D).astype(jnp.int32)


def draw_mixing(key, part):
    layer_keys = jax.random.split(jax.random.fold_in(key, 23), LAYERS)
    return jax.vmap(mixing_row_draw)(layer_keys)


def block_scale(own_key, extent, cuts, smallest, largest):
    loudness, own = 1.0, jax.random.fold_in(own_key, 6)
    for position, shards_of in cuts:
        draws = jnp.exp(jax.random.uniform(jax.random.fold_in(own, position), (shards_of,), jnp.float32, smallest / len(cuts), largest / len(cuts)))
        loudness = loudness * jnp.repeat(draws, extent[position] // shards_of).reshape([-1 if axis == position else 1 for axis in range(len(extent))])
    return loudness


def normal_values(rng, shape, deviation, most, cuts=(), held_as=jnp.bfloat16):
    values = deviation * jax.random.normal(rng, shape, jnp.float32)
    if cuts:
        values = values * block_scale(rng, shape, cuts, -0.22, 0.18)
    return jnp.clip(values, -most, most).astype(held_as)


def setup_inputs(seed: int = 0) -> dict:
    arg_keys = jax.random.split(jax.random.key(seed), 8)
    return {
        "inputs": draw_inputs(jax.random.fold_in(arg_keys[7], 71), 0),
        "cotangent": normal_values(arg_keys[1], (MICRO, TOKENS, D), 0.05, 0.29882812, ((1, 8), (2, 4))),
        "first_factor": normal_values(arg_keys[2], (LAYERS, NBLK, BLOCK, BLOCK), BLOCK ** -0.5, 0.5, ((0, 4),)),
        "second_factor": normal_values(arg_keys[3], (LAYERS, NBLK, BLOCK, BLOCK), BLOCK ** -0.5, 0.5, ((0, 4),)),
        "gains": jnp.clip(1.0 + 0.18 * jax.random.normal(arg_keys[4], (LAYERS, D), jnp.float32), 0.1, 1.9),
        "mixing": draw_mixing(jax.random.fold_in(arg_keys[7], 71), 0),
        "order": jax.random.permutation(arg_keys[6], MICRO).astype(jnp.int32),
    }


EPS = 1e-05

def block_apply(values, factor):
    row_count = values.shape[0]
    shaped = values.reshape(row_count, NBLK, BLOCK).astype(jnp.float32)
    return jnp.einsum('tbi,bij->tbj', shaped, factor.astype(jnp.float32)).reshape(row_count, D)

def block_apply_back(values, factor):
    row_count = values.shape[0]
    shaped = values.reshape(row_count, NBLK, BLOCK).astype(jnp.float32)
    return jnp.einsum('tbj,bij->tbi', shaped, factor.astype(jnp.float32)).reshape(row_count, D)

def branch_forward(hidden_in, first_block, gain_row, mixing_row):
    as_float = hidden_in.astype(jnp.float32)
    scale_inv = lax.rsqrt(lax.optimization_barrier(jnp.mean(as_float * as_float, axis=-1, keepdims=True)) + EPS)
    unit_rows = as_float * scale_inv
    normed = (unit_rows * gain_row).astype(jnp.bfloat16)
    pre_act = block_apply(normed, first_block)
    active = (pre_act * jax.nn.sigmoid(pre_act)).astype(jnp.bfloat16)
    mixed = jnp.take(active, mixing_row, axis=1)
    return (normed, unit_rows, scale_inv, pre_act, mixed)

def layer_forward(hidden_in, first_block, second_block, gain_row, mixing_row):
    pieces = branch_forward(hidden_in, first_block, gain_row, mixing_row)
    return (hidden_in.astype(jnp.float32) + block_apply(pieces[4], second_block)).astype(jnp.bfloat16)

def layer_backward(hidden_in, grad_out, first_block, second_block, gain_row, mixing_row):
    normed, unit_rows, scale_inv, pre_act, mixed = branch_forward(hidden_in, first_block, gain_row, mixing_row)
    inverse = jnp.zeros((D,), jnp.int32).at[mixing_row].set(jnp.arange(D, dtype=jnp.int32))
    grad_mixed = block_apply_back(grad_out, second_block).astype(jnp.bfloat16)
    grad_active = jnp.take(grad_mixed, inverse, axis=1)
    gate_sig = jax.nn.sigmoid(pre_act)
    grad_pre = (grad_active.astype(jnp.float32) * gate_sig * (1.0 + pre_act * (1.0 - gate_sig))).astype(jnp.bfloat16)
    grad_normed = block_apply_back(grad_pre, first_block)
    grad_unit = grad_normed * gain_row
    correction = lax.optimization_barrier(jnp.mean(grad_unit * unit_rows, axis=-1, keepdims=True))
    grad_in = (grad_out.astype(jnp.float32) + scale_inv * (grad_unit - unit_rows * correction)).astype(jnp.bfloat16)
    return (grad_in, grad_pre, normed, mixed)

def grouped(left, right):
    left_rows = left.reshape(MICRO, N_DP, TOK_MB, NBLK, BLOCK).astype(jnp.float32)
    right_rows = right.reshape(MICRO, N_DP, TOK_MB, NBLK, BLOCK).astype(jnp.float32)
    partial_sums = jnp.einsum('mgtbi,mgtbj->gbij', left_rows, right_rows)
    partial_sums = lax.optimization_barrier(partial_sums.astype(jnp.bfloat16)).astype(jnp.float32)
    return lax.optimization_barrier(jnp.sum(partial_sums, axis=0)).astype(jnp.bfloat16)

def reference(inputs, cotangent, first_factor, second_factor, gains, mixing, order):
    row_total = MICRO * TOKENS
    start_rows = jnp.take(inputs, order, axis=0).reshape(row_total, D)
    grads_top = cotangent.reshape(row_total, D)

    def forward_layer(hidden, layer_args):
        first_block, second_block, gain_row, mixing_row = layer_args
        return (layer_forward(hidden, first_block, second_block, gain_row, mixing_row), hidden)
    top_rows, stacked = lax.scan(forward_layer, start_rows, (first_factor, second_factor, gains, mixing))

    def backward_layer(grad_rows, layer_args):
        first_block, second_block, gain_row, mixing_row, hidden = layer_args
        grad_in, grad_pre, normed, mixed = layer_backward(hidden, grad_rows, first_block, second_block, gain_row, mixing_row)
        return (grad_in, (grouped(normed, grad_pre), grouped(mixed, grad_rows)))
    bottom, grads = lax.scan(backward_layer, grads_top, (first_factor, second_factor, gains, mixing, stacked), reverse=True)
    return (grads[0], grads[1])
```

```python
import functools

import jax
import jax.numpy as jnp
from jax import lax
from jax.experimental import pallas as pl
from jax.experimental.pallas import tpu as pltpu
from jax.sharding import PartitionSpec as P

EPS = 1e-05


def shifted(x, axis, by):
    devices = lax.axis_size(axis)
    pairs = [(i, i + by) for i in range(devices) if 0 <= i + by < devices]
    return lax.ppermute(x, axis, pairs)


def block_apply(values, factor):
    row_count = values.shape[0]
    shaped = values.reshape(row_count, factor.shape[0], factor.shape[1])
    return jnp.einsum("tbi,bij->tbj", shaped, factor, preferred_element_type=jnp.float32).reshape(
        row_count, -1
    )


def block_apply_back(values, factor):
    row_count = values.shape[0]
    shaped = values.reshape(row_count, factor.shape[0], factor.shape[1])
    return jnp.einsum("tbj,bij->tbi", shaped, factor, preferred_element_type=jnp.float32).reshape(
        row_count, -1
    )


def mixing_tables(mixing_row, blocks, block_size):
    block_ids = mixing_row[:blocks] // block_size
    lane_ids = mixing_row[::blocks] % block_size
    block_table = (jnp.arange(blocks, dtype=jnp.int32)[:, None] == block_ids[None, :]).astype(
        jnp.bfloat16
    )
    lane_table = (jnp.arange(block_size, dtype=jnp.int32)[:, None] == lane_ids[None, :]).astype(
        jnp.bfloat16
    )
    return (block_table, lane_table)


def mix_forward(active, tables):
    block_table, lane_table = tables
    row_count = active.shape[0]
    shaped = active.reshape(row_count, block_table.shape[0], lane_table.shape[0])
    halfway = jnp.einsum(
        "tbi,ia->tba", shaped, lane_table, preferred_element_type=jnp.float32
    ).astype(jnp.bfloat16)
    moved = jnp.einsum(
        "tba,be->tae", halfway, block_table, preferred_element_type=jnp.float32
    ).astype(jnp.bfloat16)
    return moved.reshape(row_count, -1)


def mix_backward(grad_mixed, tables):
    block_table, lane_table = tables
    row_count = grad_mixed.shape[0]
    shaped = grad_mixed.reshape(row_count, lane_table.shape[0], block_table.shape[0])
    halfway = jnp.einsum(
        "tae,be->tab", shaped, block_table, preferred_element_type=jnp.float32
    ).astype(jnp.bfloat16)
    moved = jnp.einsum(
        "tab,ia->tbi", halfway, lane_table, preferred_element_type=jnp.float32
    ).astype(jnp.bfloat16)
    return moved.reshape(row_count, -1)


def branch_forward(hidden_in, first_block, gain_row, tables):
    as_float = hidden_in.astype(jnp.float32)
    scale_inv = lax.rsqrt(jnp.mean(as_float * as_float, axis=-1, keepdims=True) + EPS)
    unit_rows = as_float * scale_inv
    normed = (unit_rows * gain_row).astype(jnp.bfloat16)
    pre_act = block_apply(normed, first_block)
    active = (pre_act * jax.nn.sigmoid(pre_act)).astype(jnp.bfloat16)
    mixed = mix_forward(active, tables)
    return (normed, unit_rows, scale_inv, pre_act, mixed)


def layer_forward(hidden_in, first_block, second_block, gain_row, tables):
    pieces = branch_forward(hidden_in, first_block, gain_row, tables)
    return (hidden_in.astype(jnp.float32) + block_apply(pieces[4], second_block)).astype(
        jnp.bfloat16
    )


def layer_backward(hidden_in, grad_out, first_block, second_block, gain_row, tables):
    normed, unit_rows, scale_inv, pre_act, mixed = branch_forward(
        hidden_in, first_block, gain_row, tables
    )
    grad_mixed = block_apply_back(grad_out, second_block).astype(jnp.bfloat16)
    grad_active = mix_backward(grad_mixed, tables)
    gate_sig = jax.nn.sigmoid(pre_act)
    grad_pre = (
        grad_active.astype(jnp.float32) * gate_sig * (1.0 + pre_act * (1.0 - gate_sig))
    ).astype(jnp.bfloat16)
    grad_normed = block_apply_back(grad_pre, first_block)
    grad_unit = grad_normed * gain_row
    correction = jnp.mean(grad_unit * unit_rows, axis=-1, keepdims=True)
    grad_in = (
        grad_out.astype(jnp.float32) + scale_inv * (grad_unit - unit_rows * correction)
    ).astype(jnp.bfloat16)
    return (grad_in, grad_pre, normed, mixed)


def keep_slot(buffer, value, slot, is_live):
    previous = lax.dynamic_index_in_dim(buffer, slot, 0, keepdims=False)
    return lax.dynamic_update_index_in_dim(buffer, jnp.where(is_live, value, previous), slot, 0)


def body(inputs, cotangent, first_factor, second_factor, gains, mixing, order):
    sections = lax.axis_size("section")
    position = lax.axis_index("section")
    micro_count = inputs.shape[0]
    row_count = inputs.shape[1]
    whole_inputs, whole_cotangent = (
        lax.all_gather(inputs, "section", axis=2, tiled=True),
        lax.all_gather(cotangent, "section", axis=2, tiled=True),
    )
    feature_count = whole_inputs.shape[2]
    first_block = first_factor[0]
    second_block = second_factor[0]
    gain_row = gains[0]
    tables = mixing_tables(mixing[0], first_block.shape[0], first_block.shape[1])
    zero_rows = jnp.zeros((row_count, feature_count), jnp.bfloat16)
    zero_stash = jnp.zeros((micro_count, row_count, feature_count), jnp.bfloat16)
    tick_count = sections + micro_count - 1

    def forward_tick(moment, state_now):
        incoming, stashed = state_now
        slot_index = moment - position
        is_live = (slot_index >= 0) & (slot_index < micro_count)
        position_in = jnp.clip(slot_index, 0, micro_count - 1)
        entering = lax.dynamic_index_in_dim(order, position_in, 0, keepdims=False)
        fed_row = lax.dynamic_index_in_dim(whole_inputs, entering, 0, keepdims=False)
        source_rows = jnp.where(position == 0, fed_row, incoming)
        result_rows = lax.cond(
            is_live,
            lambda: layer_forward(source_rows, first_block, second_block, gain_row, tables),
            lambda: zero_rows,
        )
        stashed = keep_slot(stashed, source_rows, position_in, is_live)
        incoming = shifted(result_rows, "section", 1)
        return (incoming, stashed)

    def backward_tick(moment, state_now, stashed):
        incoming, grads_out, grads_pre, normed_keep, mixed_keep = state_now
        slot_index = moment - (sections - 1 - position)
        is_live = (slot_index >= 0) & (slot_index < micro_count)
        position_in = jnp.clip(slot_index, 0, micro_count - 1)
        given_row = lax.dynamic_index_in_dim(whole_cotangent, position_in, 0, keepdims=False)
        arriving = jnp.where(position == sections - 1, given_row, incoming)
        hidden_in = lax.dynamic_index_in_dim(stashed, position_in, 0, keepdims=False)
        grad_in, grad_pre, normed, mixed = lax.cond(
            is_live,
            lambda: layer_backward(
                hidden_in, arriving, first_block, second_block, gain_row, tables
            ),
            lambda: (zero_rows, zero_rows, zero_rows, zero_rows),
        )
        grads_out = keep_slot(grads_out, arriving, position_in, is_live)
        grads_pre = keep_slot(grads_pre, grad_pre, position_in, is_live)
        normed_keep = keep_slot(normed_keep, normed, position_in, is_live)
        mixed_keep = keep_slot(mixed_keep, mixed, position_in, is_live)
        incoming = shifted(grad_in, "section", -1)
        return (incoming, grads_out, grads_pre, normed_keep, mixed_keep)

    start_forward = (zero_rows, zero_stash)
    start_backward = (zero_rows, zero_stash, zero_stash, zero_stash, zero_stash)
    forward = lax.fori_loop(0, tick_count, forward_tick, start_forward)
    stashed = forward[1]
    backward = lax.fori_loop(
        0,
        tick_count,
        lambda moment, state_now: backward_tick(moment, state_now, stashed),
        start_backward,
    )
    blocks = first_block.shape[0]
    block_size = first_block.shape[1]
    grads_out = backward[1].reshape(-1, blocks, block_size)
    grads_pre = backward[2].reshape(-1, blocks, block_size)
    normed_all = backward[3].reshape(-1, blocks, block_size)
    mixed_all = backward[4].reshape(-1, blocks, block_size)
    part_first = jnp.einsum(
        "tbi,tbj->bij", normed_all, grads_pre, preferred_element_type=jnp.float32
    )
    part_second = jnp.einsum(
        "tbi,tbj->bij", mixed_all, grads_out, preferred_element_type=jnp.float32
    )
    summed_first, summed_second = (
        lax.psum(part_first.astype(jnp.bfloat16), "dp").astype(jnp.float32),
        lax.psum(part_second.astype(jnp.bfloat16), "dp").astype(jnp.float32),
    )
    total_first = summed_first.astype(jnp.bfloat16)
    total_second = summed_second.astype(jnp.bfloat16)
    return (total_first[None], total_second[None])


MESH = pl.DeviceIdType.MESH
NT = (((1,), (1,)), ((), ()))
TN = (((0,), (0,)), ((), ()))


def rows_of(b):
    return pl.ds(pl.multiple_of(b * 128, 128), 128)


def step_kernel(
    S, NB, z0, cot, w1own, w2own, gown,
    g1, g2,
    w1, w2, grow, gcol, z, pre, act, fstage, mixed, bstage, brecv, gbuf, gpbuf, wbuf,
    ssend, srecv, rbuf,
    wlocal, wsend, wrecv, fsend, frecv, bsend, brsem, sssem, srsem,
):
    me = lax.axis_index("section")
    AC = 128 // S
    D = S * NB * 128

    def peer(d):
        return lax.rem(me + d, S)

    def remote(src, dst, send, recv, d):
        return pltpu.make_async_remote_copy(
            src_ref=src, dst_ref=dst, send_sem=send, recv_sem=recv,
            device_id={"section": peer(d)}, device_id_type=MESH,
        )

    barrier = pltpu.get_barrier_semaphore()
    for d in range(1, S):
        pl.semaphore_signal(barrier, inc=1, device_id={"section": peer(d)}, device_id_type=MESH)
    pl.semaphore_wait(barrier, S - 1)

    own = ((gown, grow), (w1own, w1), (w2own, w2))

    def weight_copy(k, d):
        src, dst = own[k]
        part = src.at[pl.ds(peer(d) * NB, NB)]
        return remote(part, dst.at[me], wsend.at[k, d - 1], wrecv.at[k, me], d)

    def weight_local(k):
        src, dst = own[k]
        return pltpu.make_async_copy(src.at[pl.ds(me * NB, NB)], dst.at[me], wrecv.at[k, me])

    def weight_wait(k, l):
        src, dst = own[k]
        pltpu.make_async_copy(src.at[pl.ds(0, NB)], dst.at[l], wrecv.at[k, l]).wait()

    for k in range(3):
        for d in range(1, S):
            weight_copy(k, d).start()
        weight_local(k).start()

    def sums_copy(k, d):
        return remote(ssend.at[k], srecv.at[k, d - 1], sssem.at[k, d - 1], srsem.at[k, d - 1], d)

    def sums_start(k, value):
        ssend[k] = jnp.broadcast_to(value, (8, 128))
        for d in range(1, S):
            sums_copy(k, d).start()

    def sums_wait(k):
        for d in range(1, S):
            sums_copy(k, d).wait()
        total = ssend[k]
        for d in range(1, S):
            total = total + srecv[k, d - 1]
        return total[0:1, :]

    def fcopy(l, d):
        return remote(
            fstage.at[l, pl.ds(peer(d) * AC, AC)], mixed.at[l, me],
            fsend.at[l, d - 1], frecv.at[l, d - 1], d,
        )

    def bcopy(l, d):
        return remote(
            bstage.at[l, peer(d)], brecv.at[l, pl.ds(me * AC, AC)],
            bsend.at[l, d - 1], brsem.at[l, d - 1], d,
        )

    def mixed_block(l, b):
        parts = [mixed[l, :, 2 * b + p].reshape(S * NB, 128) for p in range(2)]
        return jnp.concatenate(parts, axis=0)

    def back_send(l):
        def block(b, carry):
            gm = jnp.dot(w2[l, b], gbuf[rows_of(b)], preferred_element_type=jnp.float32)
            gm = gm.astype(jnp.bfloat16)
            for p in range(2):
                for s in range(S):
                    at = (p * S + s) * NB
                    bstage[l, s, 2 * b + p] = gm[at:at + NB]
            return carry
        lax.fori_loop(0, NB, block, 0, unroll=UNROLL)
        for d in range(1, S):
            bcopy(l, d).start()
        brecv[l, pl.ds(me * AC, AC)] = bstage[l, me]

    def squares(b, total):
        zb = z[0, rows_of(b)].astype(jnp.float32)
        return total + jnp.sum(zb * zb, axis=0, keepdims=True)

    zero = jnp.zeros((1, 128), jnp.float32)

    def load_z(b, carry):
        z[0, rows_of(b)] = z0[rows_of(b)]
        gbuf[rows_of(b)] = cot[rows_of(b)]
        return carry
    lax.fori_loop(0, NB, load_z, 0)
    sums_start(0, lax.fori_loop(0, NB, squares, zero))

    for l in range(S):
        weight_wait(0, l)

    def spread(q, carry):
        l = q // NB
        b = lax.rem(q, NB)
        line = jnp.broadcast_to(grow[l, pl.ds(b, 1)], (128, 128))
        gcol[l, rows_of(b)] = line.T
        return carry
    lax.fori_loop(0, S * NB, spread, 0)

    def forward(l, last):
        weight_wait(1, l)

        def first(b, carry):
            zg = (z[l, rows_of(b)].astype(jnp.float32) * gcol[l, rows_of(b)]).astype(jnp.bfloat16)
            pre[l, rows_of(b)] = lax.dot_general(
                w1[l, b], zg, TN, preferred_element_type=jnp.float32
            )
            return carry
        lax.fori_loop(0, NB, first, 0, unroll=UNROLL)
        r = lax.rsqrt(sums_wait(l) * (1.0 / D) + EPS)
        rbuf[l] = jnp.broadcast_to(r, (8, 128))

        def gate(b, carry):
            value = pre[l, rows_of(b)] * r
            pre[l, rows_of(b)] = value
            act[rows_of(b)] = value * jax.nn.sigmoid(value)
            return carry
        lax.fori_loop(0, NB, gate, 0, unroll=UNROLL)

        def pack(a, carry):
            fstage[l, a] = act[pl.ds(a, NB, stride=128), :].astype(jnp.bfloat16)
            return carry
        lax.fori_loop(0, 128, pack, 0, unroll=8)
        for d in range(1, S):
            fcopy(l, d).start()
        mixed[l, me] = fstage[l, pl.ds(me * AC, AC)]
        weight_wait(2, l)
        if last:
            back_send(l)
            for d in range(1, S):
                fcopy(l, d).wait()
            return
        for d in range(1, S):
            fcopy(l, d).wait()

        def second(b, total):
            out = lax.dot_general(
                w2[l, b], mixed_block(l, b), TN, preferred_element_type=jnp.float32
            )
            zn = (z[l, rows_of(b)].astype(jnp.float32) + out).astype(jnp.bfloat16)
            z[l + 1, rows_of(b)] = zn
            zf = zn.astype(jnp.float32)
            return total + jnp.sum(zf * zf, axis=0, keepdims=True)
        sums_start(l + 1, lax.fori_loop(0, NB, second, zero, unroll=UNROLL))

    def backward(l, last):
        def grad_second(b, carry):
            g2[l, b] = lax.dot_general(
                mixed_block(l, b), gbuf[rows_of(b)], NT, preferred_element_type=jnp.float32
            ).astype(jnp.bfloat16)
            return carry
        lax.fori_loop(0, NB, grad_second, 0, unroll=UNROLL)
        for d in range(1, S):
            bcopy(l, d).wait()

        def unpack(a, carry):
            act[pl.ds(a, NB, stride=128), :] = brecv[l, a].astype(jnp.float32)
            return carry
        lax.fori_loop(0, 128, unpack, 0, unroll=8)
        r = rbuf[l][0:1, :]

        def gate(b, total):
            value = pre[l, rows_of(b)]
            s = jax.nn.sigmoid(value)
            gp = (act[rows_of(b)] * s * (1.0 + value * (1.0 - s))).astype(jnp.bfloat16)
            gpbuf[rows_of(b)] = gp
            if last:
                return total
            w = jnp.dot(w1[l, b], gp, preferred_element_type=jnp.float32) * gcol[l, rows_of(b)]
            wbuf[rows_of(b)] = w
            u = z[l, rows_of(b)].astype(jnp.float32) * r
            return total + jnp.sum(w * u, axis=0, keepdims=True)
        total = lax.fori_loop(0, NB, gate, zero, unroll=UNROLL)
        if not last:
            sums_start(S + l, total)

        def grad_first(b, carry):
            u = z[l, rows_of(b)].astype(jnp.float32) * r
            normed = (u * gcol[l, rows_of(b)]).astype(jnp.bfloat16)
            g1[l, b] = lax.dot_general(
                normed, gpbuf[rows_of(b)], NT, preferred_element_type=jnp.float32
            ).astype(jnp.bfloat16)
            return carry
        lax.fori_loop(0, NB, grad_first, 0, unroll=UNROLL)
        if last:
            return
        c = sums_wait(S + l) * (1.0 / D)

        def grad_in(b, carry):
            u = z[l, rows_of(b)].astype(jnp.float32) * r
            gf = gbuf[rows_of(b)].astype(jnp.float32) + r * (wbuf[rows_of(b)] - u * c)
            gbuf[rows_of(b)] = gf.astype(jnp.bfloat16)
            return carry
        lax.fori_loop(0, NB, grad_in, 0, unroll=UNROLL)

    def forward_step(l, carry):
        forward(l, False)
        return carry
    lax.fori_loop(0, S - 1, forward_step, 0)
    forward(S - 1, True)

    def backward_step(k, carry):
        l = S - 1 - k
        backward(l, False)
        back_send(l - 1)
        return carry
    lax.fori_loop(0, S - 1, backward_step, 0)
    backward(0, True)

    for k in range(3):
        for d in range(1, S):
            weight_copy(k, d).wait_send()


UNROLL = 4


def local_step(S, NB, z0, cot, w1own, w2own, gown):
    F = NB * 128
    AC = 128 // S
    bf, f32 = jnp.bfloat16, jnp.float32
    vmem = pl.BlockSpec(memory_space=pltpu.VMEM)
    dma = pltpu.SemaphoreType.DMA
    shape = jax.ShapeDtypeStruct((S, NB, 128, 128), bf)
    return pl.pallas_call(
        functools.partial(step_kernel, S, NB),
        out_shape=(shape, shape),
        in_specs=[vmem] * 5,
        out_specs=(vmem, vmem),
        scratch_shapes=[
            pltpu.VMEM((S, NB, 128, 128), bf),
            pltpu.VMEM((S, NB, 128, 128), bf),
            pltpu.VMEM((S, NB, 128), f32),
            pltpu.VMEM((S, F, 128), f32),
            pltpu.VMEM((S, F, 128), bf),
            pltpu.VMEM((S, F, 128), f32),
            pltpu.VMEM((F, 128), f32),
            pltpu.VMEM((S, 128, NB, 128), bf),
            pltpu.VMEM((S, S, AC, NB, 128), bf),
            pltpu.VMEM((S, S, AC, NB, 128), bf),
            pltpu.VMEM((S, 128, NB, 128), bf),
            pltpu.VMEM((F, 128), bf),
            pltpu.VMEM((F, 128), bf),
            pltpu.VMEM((F, 128), f32),
            pltpu.VMEM((2 * S, 8, 128), f32),
            pltpu.VMEM((2 * S, S - 1, 8, 128), f32),
            pltpu.VMEM((S, 8, 128), f32),
            dma((1,)),
            dma((3, S - 1)),
            dma((3, S)),
            dma((S, S - 1)),
            dma((S, S - 1)),
            dma((S, S - 1)),
            dma((S, S - 1)),
            dma((2 * S, S - 1)),
            dma((2 * S, S - 1)),
        ],
        compiler_params=pltpu.CompilerParams(
            collective_id=0, has_side_effects=True, vmem_limit_bytes=58 * 1024 * 1024
        ),
        name="step",
    )(z0, cot, w1own, w2own, gown)


def fast_body(inputs, cotangent, first_factor, second_factor, gains, mixing, order):
    sections = lax.axis_size("section")
    first_block, second_block = first_factor[0], second_factor[0]
    blocks, size = first_block.shape[0], first_block.shape[1]
    NB = blocks // sections
    block_table, lane_table = mixing_tables(mixing[0], blocks, size)
    w1p = jnp.einsum(
        "bij,ja->bia", first_block, lane_table, preferred_element_type=jnp.float32
    ).astype(jnp.bfloat16)
    w2p = jnp.einsum(
        "be,qpej->qpbj", block_table, second_block.reshape(blocks, 2, blocks, size),
        preferred_element_type=jnp.float32,
    ).astype(jnp.bfloat16).reshape(blocks, size, size)
    rows = inputs.shape[0] * inputs.shape[1]
    z0 = jnp.take(inputs, order, axis=0).reshape(rows, -1).T
    cot = cotangent.reshape(rows, -1).T
    g1, g2 = local_step(sections, NB, z0, cot, w1p, w2p, gains[0].reshape(blocks, size))
    part = jnp.stack([g1, g2], axis=1)
    part = lax.all_to_all(part, "section", split_axis=0, concat_axis=0, tiled=True)
    total = lax.psum(part, "dp")
    t1 = total[:, 0].reshape(blocks, size, size)
    t2 = total[:, 1].reshape(blocks, 2, blocks, size)
    out1 = jnp.einsum(
        "bia,ja->bij", t1, lane_table, preferred_element_type=jnp.float32
    ).astype(jnp.bfloat16)
    out2 = jnp.einsum(
        "be,qpbj->qpej", block_table, t2, preferred_element_type=jnp.float32
    ).astype(jnp.bfloat16).reshape(blocks, size, size)
    return (out1[None], out2[None])


def solution(mesh):
    quick = mesh.shape["section"] == 4
    return jax.shard_map(
        fast_body if quick else body,
        mesh=mesh,
        in_specs=(
            P(None, "dp", "section"),
            P(None, "dp", "section"),
            P("section", None, None, None),
            P("section", None, None, None),
            P("section", None),
            P("section", None),
            P(),
        ),
        out_specs=(P("section", None, None, None), P("section", None, None, None)),
        check_vma=False,
    )
```

```python
import functools

import jax
import jax.numpy as jnp
from jax import lax
from jax.experimental import pallas as pl
from jax.experimental.pallas import tpu as pltpu
from jax.sharding import PartitionSpec as P

EPS = 1e-05


def shifted(x, axis, by):
    devices = lax.axis_size(axis)
    pairs = [(i, i + by) for i in range(devices) if 0 <= i + by < devices]
    return lax.ppermute(x, axis, pairs)


def block_apply(values, factor):
    row_count = values.shape[0]
    shaped = values.reshape(row_count, factor.shape[0], factor.shape[1])
    return jnp.einsum("tbi,bij->tbj", shaped, factor, preferred_element_type=jnp.float32).reshape(
        row_count, -1
    )


def block_apply_back(values, factor):
    row_count = values.shape[0]
    shaped = values.reshape(row_count, factor.shape[0], factor.shape[1])
    return jnp.einsum("tbj,bij->tbi", shaped, factor, preferred_element_type=jnp.float32).reshape(
        row_count, -1
    )


def mixing_tables(mixing_row, blocks, block_size):
    block_ids = mixing_row[:blocks] // block_size
    lane_ids = mixing_row[::blocks] % block_size
    block_table = (jnp.arange(blocks, dtype=jnp.int32)[:, None] == block_ids[None, :]).astype(
        jnp.bfloat16
    )
    lane_table = (jnp.arange(block_size, dtype=jnp.int32)[:, None] == lane_ids[None, :]).astype(
        jnp.bfloat16
    )
    return (block_table, lane_table)


def mix_forward(active, tables):
    block_table, lane_table = tables
    row_count = active.shape[0]
    shaped = active.reshape(row_count, block_table.shape[0], lane_table.shape[0])
    halfway = jnp.einsum(
        "tbi,ia->tba", shaped, lane_table, preferred_element_type=jnp.float32
    ).astype(jnp.bfloat16)
    moved = jnp.einsum(
        "tba,be->tae", halfway, block_table, preferred_element_type=jnp.float32
    ).astype(jnp.bfloat16)
    return moved.reshape(row_count, -1)


def mix_backward(grad_mixed, tables):
    block_table, lane_table = tables
    row_count = grad_mixed.shape[0]
    shaped = grad_mixed.reshape(row_count, lane_table.shape[0], block_table.shape[0])
    halfway = jnp.einsum(
        "tae,be->tab", shaped, block_table, preferred_element_type=jnp.float32
    ).astype(jnp.bfloat16)
    moved = jnp.einsum(
        "tab,ia->tbi", halfway, lane_table, preferred_element_type=jnp.float32
    ).astype(jnp.bfloat16)
    return moved.reshape(row_count, -1)


def branch_forward(hidden_in, first_block, gain_row, tables):
    as_float = hidden_in.astype(jnp.float32)
    scale_inv = lax.rsqrt(jnp.mean(as_float * as_float, axis=-1, keepdims=True) + EPS)
    unit_rows = as_float * scale_inv
    normed = (unit_rows * gain_row).astype(jnp.bfloat16)
    pre_act = block_apply(normed, first_block)
    active = (pre_act * jax.nn.sigmoid(pre_act)).astype(jnp.bfloat16)
    mixed = mix_forward(active, tables)
    return (normed, unit_rows, scale_inv, pre_act, mixed)


def layer_forward(hidden_in, first_block, second_block, gain_row, tables):
    pieces = branch_forward(hidden_in, first_block, gain_row, tables)
    return (hidden_in.astype(jnp.float32) + block_apply(pieces[4], second_block)).astype(
        jnp.bfloat16
    )


def layer_backward(hidden_in, grad_out, first_block, second_block, gain_row, tables):
    normed, unit_rows, scale_inv, pre_act, mixed = branch_forward(
        hidden_in, first_block, gain_row, tables
    )
    grad_mixed = block_apply_back(grad_out, second_block).astype(jnp.bfloat16)
    grad_active = mix_backward(grad_mixed, tables)
    gate_sig = jax.nn.sigmoid(pre_act)
    grad_pre = (
        grad_active.astype(jnp.float32) * gate_sig * (1.0 + pre_act * (1.0 - gate_sig))
    ).astype(jnp.bfloat16)
    grad_normed = block_apply_back(grad_pre, first_block)
    grad_unit = grad_normed * gain_row
    correction = jnp.mean(grad_unit * unit_rows, axis=-1, keepdims=True)
    grad_in = (
        grad_out.astype(jnp.float32) + scale_inv * (grad_unit - unit_rows * correction)
    ).astype(jnp.bfloat16)
    return (grad_in, grad_pre, normed, mixed)


def keep_slot(buffer, value, slot, is_live):
    previous = lax.dynamic_index_in_dim(buffer, slot, 0, keepdims=False)
    return lax.dynamic_update_index_in_dim(buffer, jnp.where(is_live, value, previous), slot, 0)


def body(inputs, cotangent, first_factor, second_factor, gains, mixing, order):
    sections = lax.axis_size("section")
    position = lax.axis_index("section")
    micro_count = inputs.shape[0]
    row_count = inputs.shape[1]
    whole_inputs, whole_cotangent = (
        lax.all_gather(inputs, "section", axis=2, tiled=True),
        lax.all_gather(cotangent, "section", axis=2, tiled=True),
    )
    feature_count = whole_inputs.shape[2]
    first_block = first_factor[0]
    second_block = second_factor[0]
    gain_row = gains[0]
    tables = mixing_tables(mixing[0], first_block.shape[0], first_block.shape[1])
    zero_rows = jnp.zeros((row_count, feature_count), jnp.bfloat16)
    zero_stash = jnp.zeros((micro_count, row_count, feature_count), jnp.bfloat16)
    tick_count = sections + micro_count - 1

    def forward_tick(moment, state_now):
        incoming, stashed = state_now
        slot_index = moment - position
        is_live = (slot_index >= 0) & (slot_index < micro_count)
        position_in = jnp.clip(slot_index, 0, micro_count - 1)
        entering = lax.dynamic_index_in_dim(order, position_in, 0, keepdims=False)
        fed_row = lax.dynamic_index_in_dim(whole_inputs, entering, 0, keepdims=False)
        source_rows = jnp.where(position == 0, fed_row, incoming)
        result_rows = lax.cond(
            is_live,
            lambda: layer_forward(source_rows, first_block, second_block, gain_row, tables),
            lambda: zero_rows,
        )
        stashed = keep_slot(stashed, source_rows, position_in, is_live)
        incoming = shifted(result_rows, "section", 1)
        return (incoming, stashed)

    def backward_tick(moment, state_now, stashed):
        incoming, grads_out, grads_pre, normed_keep, mixed_keep = state_now
        slot_index = moment - (sections - 1 - position)
        is_live = (slot_index >= 0) & (slot_index < micro_count)
        position_in = jnp.clip(slot_index, 0, micro_count - 1)
        given_row = lax.dynamic_index_in_dim(whole_cotangent, position_in, 0, keepdims=False)
        arriving = jnp.where(position == sections - 1, given_row, incoming)
        hidden_in = lax.dynamic_index_in_dim(stashed, position_in, 0, keepdims=False)
        grad_in, grad_pre, normed, mixed = lax.cond(
            is_live,
            lambda: layer_backward(
                hidden_in, arriving, first_block, second_block, gain_row, tables
            ),
            lambda: (zero_rows, zero_rows, zero_rows, zero_rows),
        )
        grads_out = keep_slot(grads_out, arriving, position_in, is_live)
        grads_pre = keep_slot(grads_pre, grad_pre, position_in, is_live)
        normed_keep = keep_slot(normed_keep, normed, position_in, is_live)
        mixed_keep = keep_slot(mixed_keep, mixed, position_in, is_live)
        incoming = shifted(grad_in, "section", -1)
        return (incoming, grads_out, grads_pre, normed_keep, mixed_keep)

    start_forward = (zero_rows, zero_stash)
    start_backward = (zero_rows, zero_stash, zero_stash, zero_stash, zero_stash)
    forward = lax.fori_loop(0, tick_count, forward_tick, start_forward)
    stashed = forward[1]
    backward = lax.fori_loop(
        0,
        tick_count,
        lambda moment, state_now: backward_tick(moment, state_now, stashed),
        start_backward,
    )
    blocks = first_block.shape[0]
    block_size = first_block.shape[1]
    grads_out = backward[1].reshape(-1, blocks, block_size)
    grads_pre = backward[2].reshape(-1, blocks, block_size)
    normed_all = backward[3].reshape(-1, blocks, block_size)
    mixed_all = backward[4].reshape(-1, blocks, block_size)
    part_first = jnp.einsum(
        "tbi,tbj->bij", normed_all, grads_pre, preferred_element_type=jnp.float32
    )
    part_second = jnp.einsum(
        "tbi,tbj->bij", mixed_all, grads_out, preferred_element_type=jnp.float32
    )
    summed_first, summed_second = (
        lax.psum(part_first.astype(jnp.bfloat16), "dp").astype(jnp.float32),
        lax.psum(part_second.astype(jnp.bfloat16), "dp").astype(jnp.float32),
    )
    total_first = summed_first.astype(jnp.bfloat16)
    total_second = summed_second.astype(jnp.bfloat16)
    return (total_first[None], total_second[None])


MESH = pl.DeviceIdType.MESH
NT = (((1,), (1,)), ((), ()))
TN = (((0,), (0,)), ((), ()))


def rows_of(b):
    return pl.ds(pl.multiple_of(b * 128, 128), 128)


def step_kernel(
    S, NZ, NB, z0, cot, w1own, w2own, gown,
    out,
    w1, w2, grow, gcol, z, pre, act, fstage, mixed, bstage, brecv, gbuf, gpbuf, wbuf,
    ssend, srecv, rbuf, gsend, arecv, bsum, zrecv, csum, gath,
    wsend, wrecv, fsend, frecv, bsend, brsem, sssem, srsem,
    asend, arsem, zsend, zrsem, csend, crsem, dsend, drsem, esend, ersem, osem,
):
    me = lax.axis_index("section")
    at = lax.axis_index("dp")
    mz, my = at // 2, lax.rem(at, 2)
    half = NB // 2
    per = half // NZ
    AC = 128 // S
    D = S * NB * 128

    def peer(d):
        return lax.rem(me + d, S)

    def z_at(d):
        return lax.rem(mz + d, NZ)

    def z_peer(d):
        return {"dp": z_at(d) * 2 + my}

    def remote_to(src, dst, send, recv, device):
        return pltpu.make_async_remote_copy(
            src_ref=src, dst_ref=dst, send_sem=send, recv_sem=recv,
            device_id=device, device_id_type=MESH,
        )

    def remote(src, dst, send, recv, d):
        return remote_to(src, dst, send, recv, {"section": peer(d)})

    barrier = pltpu.get_barrier_semaphore()
    for d in range(1, S):
        pl.semaphore_signal(barrier, inc=1, device_id={"section": peer(d)}, device_id_type=MESH)
    y_peer = {"dp": mz * 2 + 1 - my}
    pl.semaphore_signal(barrier, inc=1, device_id=y_peer, device_id_type=MESH)
    for d in range(1, NZ):
        pl.semaphore_signal(barrier, inc=1, device_id=z_peer(d), device_id_type=MESH)
    pl.semaphore_wait(barrier, S + NZ - 1)

    own = ((gown, grow), (w1own, w1), (w2own, w2))

    def weight_copy(k, d):
        src, dst = own[k]
        part = src.at[pl.ds(peer(d) * NB, NB)]
        return remote(part, dst.at[me], wsend.at[k, d - 1], wrecv.at[k, me], d)

    def weight_local(k):
        src, dst = own[k]
        return pltpu.make_async_copy(src.at[pl.ds(me * NB, NB)], dst.at[me], wrecv.at[k, me])

    def weight_wait(k, l):
        src, dst = own[k]
        pltpu.make_async_copy(src.at[pl.ds(0, NB)], dst.at[l], wrecv.at[k, l]).wait()

    for k in range(3):
        for d in range(1, S):
            weight_copy(k, d).start()
        weight_local(k).start()

    def sums_copy(k, d):
        return remote(ssend.at[k], srecv.at[k, d - 1], sssem.at[k, d - 1], srsem.at[k, d - 1], d)

    def sums_start(k, value):
        ssend[k] = jnp.broadcast_to(value, (8, 128))
        for d in range(1, S):
            sums_copy(k, d).start()

    def sums_wait(k):
        for d in range(1, S):
            sums_copy(k, d).wait()
        total = ssend[k]
        for d in range(1, S):
            total = total + srecv[k, d - 1]
        return total[0:1, :]

    def fcopy(l, d):
        return remote(
            fstage.at[l, pl.ds(peer(d) * AC, AC)], mixed.at[l, me],
            fsend.at[l, d - 1], frecv.at[l, d - 1], d,
        )

    def bcopy(l, d):
        return remote(
            bstage.at[l, peer(d)], brecv.at[l, pl.ds(me * AC, AC)],
            bsend.at[l, d - 1], brsem.at[l, d - 1], d,
        )

    def mixed_block(l, b):
        parts = [mixed[l, :, 2 * b + p].reshape(S * NB, 128) for p in range(2)]
        return jnp.concatenate(parts, axis=0)

    def back_send(l):
        def block(b, carry):
            gm = jnp.dot(w2[l, b], gbuf[rows_of(b)], preferred_element_type=jnp.float32)
            gm = gm.astype(jnp.bfloat16)
            for p in range(2):
                for s in range(S):
                    at = (p * S + s) * NB
                    bstage[l, s, 2 * b + p] = gm[at:at + NB]
            return carry
        lax.fori_loop(0, NB, block, 0, unroll=UNROLL)
        for d in range(1, S):
            bcopy(l, d).start()
        brecv[l, pl.ds(me * AC, AC)] = bstage[l, me]

    def squares(b, total):
        zb = z[0, rows_of(b)].astype(jnp.float32)
        return total + jnp.sum(zb * zb, axis=0, keepdims=True)

    zero = jnp.zeros((1, 128), jnp.float32)

    def load_z(b, carry):
        z[0, rows_of(b)] = z0[rows_of(b)]
        gbuf[rows_of(b)] = cot[rows_of(b)]
        return carry
    lax.fori_loop(0, NB, load_z, 0)
    sums_start(0, lax.fori_loop(0, NB, squares, zero))

    for l in range(S):
        weight_wait(0, l)

    def spread(q, carry):
        l = q // NB
        b = lax.rem(q, NB)
        line = jnp.broadcast_to(grow[l, pl.ds(b, 1)], (128, 128))
        gcol[l, rows_of(b)] = line.T
        return carry
    lax.fori_loop(0, S * NB, spread, 0)

    def forward(l, last):
        weight_wait(1, l)

        def first(b, carry):
            zg = (z[l, rows_of(b)].astype(jnp.float32) * gcol[l, rows_of(b)]).astype(jnp.bfloat16)
            pre[l, rows_of(b)] = lax.dot_general(
                w1[l, b], zg, TN, preferred_element_type=jnp.float32
            )
            return carry
        lax.fori_loop(0, NB, first, 0, unroll=UNROLL)
        r = lax.rsqrt(sums_wait(l) * (1.0 / D) + EPS)
        rbuf[l] = jnp.broadcast_to(r, (8, 128))

        def gate(b, carry):
            value = pre[l, rows_of(b)] * r
            pre[l, rows_of(b)] = value
            act[rows_of(b)] = value * jax.nn.sigmoid(value)
            return carry
        lax.fori_loop(0, NB, gate, 0, unroll=UNROLL)

        def pack(a, carry):
            fstage[l, a] = act[pl.ds(a, NB, stride=128), :].astype(jnp.bfloat16)
            return carry
        lax.fori_loop(0, 128, pack, 0, unroll=8)
        for d in range(1, S):
            fcopy(l, d).start()
        mixed[l, me] = fstage[l, pl.ds(me * AC, AC)]
        weight_wait(2, l)
        if last:
            back_send(l)
            for d in range(1, S):
                fcopy(l, d).wait()
            return
        for d in range(1, S):
            fcopy(l, d).wait()

        def second(b, total):
            out = lax.dot_general(
                w2[l, b], mixed_block(l, b), TN, preferred_element_type=jnp.float32
            )
            zn = (z[l, rows_of(b)].astype(jnp.float32) + out).astype(jnp.bfloat16)
            z[l + 1, rows_of(b)] = zn
            zf = zn.astype(jnp.float32)
            return total + jnp.sum(zf * zf, axis=0, keepdims=True)
        sums_start(l + 1, lax.fori_loop(0, NB, second, zero, unroll=UNROLL))

    def a_copy(l, f):
        return remote_to(
            gsend.at[l, f, 1 - my], arecv.at[l, f], asend.at[l, f], arsem.at[l, f], y_peer
        )

    def b_copy(l, f, d):
        return remote_to(
            bsum.at[l, f, pl.ds(z_at(d) * per, per)], zrecv.at[l, f, d - 1],
            zsend.at[l, f, d - 1], zrsem.at[l, f, d - 1], z_peer(d),
        )

    def c_copy(l, f):
        return remote_to(
            csum.at[l, f], gath.at[f, me, my, mz], csend.at[l, f], crsem.at[f, me], {"section": l}
        )

    def d_copy(f, d):
        part = gath.at[f, :, my, mz]
        return remote_to(part, part, dsend.at[f, d - 1], drsem.at[f, d - 1], z_peer(d))

    def e_copy(f, d):
        part = gath.at[f, :, my, lax.rem(mz + NZ - d, NZ)]
        return remote_to(part, part, esend.at[f, d], ersem.at[f, d], y_peer)

    def stage_b(l, f):
        a_copy(l, f).wait_recv()

        def tile(i, carry):
            total = gsend[l, f, my, i].astype(jnp.float32) + arecv[l, f, i].astype(jnp.float32)
            bsum[l, f, i] = total.astype(jnp.bfloat16)
            return carry
        lax.fori_loop(0, half, tile, 0)
        for d in range(1, NZ):
            b_copy(l, f, d).start()

    def stage_c(l, f):
        for d in range(1, NZ):
            b_copy(l, f, d).wait_recv()
        for i in range(per):
            total = bsum[l, f, mz * per + i].astype(jnp.float32)
            for d in range(1, NZ):
                total = total + zrecv[l, f, d - 1, i].astype(jnp.float32)
            csum[l, f, i] = total.astype(jnp.bfloat16)

        @pl.when(me == l)
        def _():
            gath[f, me, my, mz] = csum[l, f]

        @pl.when(me != l)
        def _():
            c_copy(l, f).start()

    def stage_d(l, f):
        @pl.when(me == l)
        def _():
            for d in range(1, S):
                part = gath.at[f, peer(d), my, mz]
                pltpu.make_async_copy(csum.at[l, f], part, crsem.at[f, peer(d)]).wait()
            for d in range(1, NZ):
                d_copy(f, d).start()
            e_copy(f, 0).start()

    def stage_e(l, f):
        @pl.when(me == l)
        def _():
            for d in range(1, NZ):
                d_copy(f, d).wait_recv()
                e_copy(f, d).start()

    def both(stage, l):
        for f in (1, 0):
            stage(l, f)

    def backward(l, last):
        def grad_second(b, carry):
            gsend[l, 1, b // half, lax.rem(b, half)] = lax.dot_general(
                mixed_block(l, b), gbuf[rows_of(b)], NT, preferred_element_type=jnp.float32
            ).astype(jnp.bfloat16)
            return carry
        lax.fori_loop(0, NB, grad_second, 0, unroll=UNROLL)
        a_copy(l, 1).start()

        @pl.when(l < S - 1)
        def _():
            both(stage_b, l + 1)

        @pl.when(l < S - 2)
        def _():
            both(stage_d, l + 2)
        for d in range(1, S):
            bcopy(l, d).wait()

        def unpack(a, carry):
            act[pl.ds(a, NB, stride=128), :] = brecv[l, a].astype(jnp.float32)
            return carry
        lax.fori_loop(0, 128, unpack, 0, unroll=8)
        r = rbuf[l][0:1, :]

        def gate(b, total):
            value = pre[l, rows_of(b)]
            s = jax.nn.sigmoid(value)
            gp = (act[rows_of(b)] * s * (1.0 + value * (1.0 - s))).astype(jnp.bfloat16)
            gpbuf[rows_of(b)] = gp
            if last:
                return total
            w = jnp.dot(w1[l, b], gp, preferred_element_type=jnp.float32) * gcol[l, rows_of(b)]
            wbuf[rows_of(b)] = w
            u = z[l, rows_of(b)].astype(jnp.float32) * r
            return total + jnp.sum(w * u, axis=0, keepdims=True)
        total = lax.fori_loop(0, NB, gate, zero, unroll=UNROLL)
        if not last:
            sums_start(S + l, total)

        def grad_first(b, carry):
            u = z[l, rows_of(b)].astype(jnp.float32) * r
            normed = (u * gcol[l, rows_of(b)]).astype(jnp.bfloat16)
            gsend[l, 0, b // half, lax.rem(b, half)] = lax.dot_general(
                normed, gpbuf[rows_of(b)], NT, preferred_element_type=jnp.float32
            ).astype(jnp.bfloat16)
            return carry
        lax.fori_loop(0, NB, grad_first, 0, unroll=UNROLL)
        a_copy(l, 0).start()

        @pl.when(l < S - 1)
        def _():
            both(stage_c, l + 1)

        @pl.when(l < S - 2)
        def _():
            both(stage_e, l + 2)
        if last:
            return
        c = sums_wait(S + l) * (1.0 / D)

        def grad_in(b, carry):
            u = z[l, rows_of(b)].astype(jnp.float32) * r
            gf = gbuf[rows_of(b)].astype(jnp.float32) + r * (wbuf[rows_of(b)] - u * c)
            gbuf[rows_of(b)] = gf.astype(jnp.bfloat16)
            return carry
        lax.fori_loop(0, NB, grad_in, 0, unroll=UNROLL)

    def forward_step(l, carry):
        forward(l, False)
        return carry
    lax.fori_loop(0, S - 1, forward_step, 0)
    forward(S - 1, True)

    def backward_step(k, carry):
        l = S - 1 - k
        backward(l, False)
        back_send(l - 1)
        return carry
    lax.fori_loop(0, S - 1, backward_step, 0)
    backward(0, True)
    stage_b(0, 1)
    both(stage_d, 1)
    stage_b(0, 0)
    both(stage_e, 1)
    both(stage_c, 0)
    both(stage_d, 0)
    both(stage_e, 0)
    for f in range(2):
        for d in range(NZ):
            e_copy(f, d).wait_recv()
    done = pltpu.make_async_copy(gath, out, osem.at[0])
    done.start()

    def finish(l, carry):
        for f in range(2):
            a_copy(l, f).wait_send()
            for d in range(1, NZ):
                b_copy(l, f, d).wait_send()

            @pl.when(me != l)
            def _():
                c_copy(l, f).wait_send()
        return carry
    lax.fori_loop(0, S, finish, 0)
    for f in range(2):
        for d in range(1, NZ):
            d_copy(f, d).wait_send()
        for d in range(NZ):
            e_copy(f, d).wait_send()
    done.wait()

    for k in range(3):
        for d in range(1, S):
            weight_copy(k, d).wait_send()


UNROLL = 4


def local_step(S, NZ, NB, z0, cot, w1own, w2own, gown):
    F = NB * 128
    AC = 128 // S
    bf, f32 = jnp.bfloat16, jnp.float32
    vmem = pl.BlockSpec(memory_space=pltpu.VMEM)
    dma = pltpu.SemaphoreType.DMA
    half = NB // 2
    per = half // NZ
    shape = jax.ShapeDtypeStruct((2, S, 2, NZ, per, 128, 128), bf)
    return pl.pallas_call(
        functools.partial(step_kernel, S, NZ, NB),
        out_shape=shape,
        in_specs=[vmem] * 5,
        out_specs=pl.BlockSpec(memory_space=pl.ANY),
        scratch_shapes=[
            pltpu.VMEM((S, NB, 128, 128), bf),
            pltpu.VMEM((S, NB, 128, 128), bf),
            pltpu.VMEM((S, NB, 128), f32),
            pltpu.VMEM((S, F, 128), f32),
            pltpu.VMEM((S, F, 128), bf),
            pltpu.VMEM((S, F, 128), f32),
            pltpu.VMEM((F, 128), f32),
            pltpu.VMEM((S, 128, NB, 128), bf),
            pltpu.VMEM((S, S, AC, NB, 128), bf),
            pltpu.VMEM((S, S, AC, NB, 128), bf),
            pltpu.VMEM((S, 128, NB, 128), bf),
            pltpu.VMEM((F, 128), bf),
            pltpu.VMEM((F, 128), bf),
            pltpu.VMEM((F, 128), f32),
            pltpu.VMEM((2 * S, 8, 128), f32),
            pltpu.VMEM((2 * S, S - 1, 8, 128), f32),
            pltpu.VMEM((S, 8, 128), f32),
            pltpu.VMEM((S, 2, 2, half, 128, 128), bf),
            pltpu.VMEM((S, 2, half, 128, 128), bf),
            pltpu.VMEM((S, 2, half, 128, 128), bf),
            pltpu.VMEM((S, 2, NZ - 1, per, 128, 128), bf),
            pltpu.VMEM((S, 2, per, 128, 128), bf),
            pltpu.VMEM((2, S, 2, NZ, per, 128, 128), bf),
            dma((3, S - 1)),
            dma((3, S)),
            dma((S, S - 1)),
            dma((S, S - 1)),
            dma((S, S - 1)),
            dma((S, S - 1)),
            dma((2 * S, S - 1)),
            dma((2 * S, S - 1)),
            dma((S, 2)),
            dma((S, 2)),
            dma((S, 2, NZ - 1)),
            dma((S, 2, NZ - 1)),
            dma((S, 2)),
            dma((2, S)),
            dma((2, NZ - 1)),
            dma((2, NZ - 1)),
            dma((2, NZ)),
            dma((2, NZ)),
            dma((1,)),
        ],
        compiler_params=pltpu.CompilerParams(
            collective_id=0, has_side_effects=True, vmem_limit_bytes=58 * 1024 * 1024
        ),
        name="step",
    )(z0, cot, w1own, w2own, gown)


def fast_body(inputs, cotangent, first_factor, second_factor, gains, mixing, order):
    sections = lax.axis_size("section")
    first_block, second_block = first_factor[0], second_factor[0]
    blocks, size = first_block.shape[0], first_block.shape[1]
    NB = blocks // sections
    block_table, lane_table = mixing_tables(mixing[0], blocks, size)
    w1p = jnp.einsum(
        "bij,ja->bia", first_block, lane_table, preferred_element_type=jnp.float32
    ).astype(jnp.bfloat16)
    w2p = jnp.einsum(
        "be,qpej->qpbj", block_table, second_block.reshape(blocks, 2, blocks, size),
        preferred_element_type=jnp.float32,
    ).astype(jnp.bfloat16).reshape(blocks, size, size)
    rows = inputs.shape[0] * inputs.shape[1]
    z0 = jnp.take(inputs, order, axis=0).reshape(rows, -1).T
    cot = cotangent.reshape(rows, -1).T
    total = local_step(
        sections, lax.axis_size("dp") // 2, NB, z0, cot, w1p, w2p, gains[0].reshape(blocks, size)
    )
    t1 = total[0].reshape(blocks, size, size)
    t2 = total[1].reshape(blocks, 2, blocks, size)
    out1 = jnp.einsum(
        "bia,ja->bij", t1, lane_table, preferred_element_type=jnp.float32
    ).astype(jnp.bfloat16)
    out2 = jnp.einsum(
        "be,qpbj->qpej", block_table, t2, preferred_element_type=jnp.float32
    ).astype(jnp.bfloat16).reshape(blocks, size, size)
    return (out1[None], out2[None])


def solution(mesh):
    quick = mesh.shape["section"] == 4 and mesh.shape["dp"] == 8
    return jax.shard_map(
        fast_body if quick else body,
        mesh=mesh,
        in_specs=(
            P(None, "dp", "section"),
            P(None, "dp", "section"),
            P("section", None, None, None),
            P("section", None, None, None),
            P("section", None),
            P("section", None),
            P(),
        ),
        out_specs=(P("section", None, None, None), P("section", None, None, None)),
        check_vma=False,
    )
```

```python
import functools

import jax
import jax.numpy as jnp
from jax import lax
from jax.experimental import pallas as pl
from jax.experimental.pallas import tpu as pltpu
from jax.sharding import PartitionSpec as P

EPS = 1e-05


def shifted(x, axis, by):
    devices = lax.axis_size(axis)
    pairs = [(i, i + by) for i in range(devices) if 0 <= i + by < devices]
    return lax.ppermute(x, axis, pairs)


def block_apply(values, factor):
    row_count = values.shape[0]
    shaped = values.reshape(row_count, factor.shape[0], factor.shape[1])
    return jnp.einsum("tbi,bij->tbj", shaped, factor, preferred_element_type=jnp.float32).reshape(
        row_count, -1
    )


def block_apply_back(values, factor):
    row_count = values.shape[0]
    shaped = values.reshape(row_count, factor.shape[0], factor.shape[1])
    return jnp.einsum("tbj,bij->tbi", shaped, factor, preferred_element_type=jnp.float32).reshape(
        row_count, -1
    )


def mixing_tables(mixing_row, blocks, block_size):
    block_ids = mixing_row[:blocks] // block_size
    lane_ids = mixing_row[::blocks] % block_size
    block_table = (jnp.arange(blocks, dtype=jnp.int32)[:, None] == block_ids[None, :]).astype(
        jnp.bfloat16
    )
    lane_table = (jnp.arange(block_size, dtype=jnp.int32)[:, None] == lane_ids[None, :]).astype(
        jnp.bfloat16
    )
    return (block_table, lane_table)


def mix_forward(active, tables):
    block_table, lane_table = tables
    row_count = active.shape[0]
    shaped = active.reshape(row_count, block_table.shape[0], lane_table.shape[0])
    halfway = jnp.einsum(
        "tbi,ia->tba", shaped, lane_table, preferred_element_type=jnp.float32
    ).astype(jnp.bfloat16)
    moved = jnp.einsum(
        "tba,be->tae", halfway, block_table, preferred_element_type=jnp.float32
    ).astype(jnp.bfloat16)
    return moved.reshape(row_count, -1)


def mix_backward(grad_mixed, tables):
    block_table, lane_table = tables
    row_count = grad_mixed.shape[0]
    shaped = grad_mixed.reshape(row_count, lane_table.shape[0], block_table.shape[0])
    halfway = jnp.einsum(
        "tae,be->tab", shaped, block_table, preferred_element_type=jnp.float32
    ).astype(jnp.bfloat16)
    moved = jnp.einsum(
        "tab,ia->tbi", halfway, lane_table, preferred_element_type=jnp.float32
    ).astype(jnp.bfloat16)
    return moved.reshape(row_count, -1)


def branch_forward(hidden_in, first_block, gain_row, tables):
    as_float = hidden_in.astype(jnp.float32)
    scale_inv = lax.rsqrt(jnp.mean(as_float * as_float, axis=-1, keepdims=True) + EPS)
    unit_rows = as_float * scale_inv
    normed = (unit_rows * gain_row).astype(jnp.bfloat16)
    pre_act = block_apply(normed, first_block)
    active = (pre_act * jax.nn.sigmoid(pre_act)).astype(jnp.bfloat16)
    mixed = mix_forward(active, tables)
    return (normed, unit_rows, scale_inv, pre_act, mixed)


def layer_forward(hidden_in, first_block, second_block, gain_row, tables):
    pieces = branch_forward(hidden_in, first_block, gain_row, tables)
    return (hidden_in.astype(jnp.float32) + block_apply(pieces[4], second_block)).astype(
        jnp.bfloat16
    )


def layer_backward(hidden_in, grad_out, first_block, second_block, gain_row, tables):
    normed, unit_rows, scale_inv, pre_act, mixed = branch_forward(
        hidden_in, first_block, gain_row, tables
    )
    grad_mixed = block_apply_back(grad_out, second_block).astype(jnp.bfloat16)
    grad_active = mix_backward(grad_mixed, tables)
    gate_sig = jax.nn.sigmoid(pre_act)
    grad_pre = (
        grad_active.astype(jnp.float32) * gate_sig * (1.0 + pre_act * (1.0 - gate_sig))
    ).astype(jnp.bfloat16)
    grad_normed = block_apply_back(grad_pre, first_block)
    grad_unit = grad_normed * gain_row
    correction = jnp.mean(grad_unit * unit_rows, axis=-1, keepdims=True)
    grad_in = (
        grad_out.astype(jnp.float32) + scale_inv * (grad_unit - unit_rows * correction)
    ).astype(jnp.bfloat16)
    return (grad_in, grad_pre, normed, mixed)


def keep_slot(buffer, value, slot, is_live):
    previous = lax.dynamic_index_in_dim(buffer, slot, 0, keepdims=False)
    return lax.dynamic_update_index_in_dim(buffer, jnp.where(is_live, value, previous), slot, 0)


def body(inputs, cotangent, first_factor, second_factor, gains, mixing, order):
    sections = lax.axis_size("section")
    position = lax.axis_index("section")
    micro_count = inputs.shape[0]
    row_count = inputs.shape[1]
    whole_inputs, whole_cotangent = (
        lax.all_gather(inputs, "section", axis=2, tiled=True),
        lax.all_gather(cotangent, "section", axis=2, tiled=True),
    )
    feature_count = whole_inputs.shape[2]
    first_block = first_factor[0]
    second_block = second_factor[0]
    gain_row = gains[0]
    tables = mixing_tables(mixing[0], first_block.shape[0], first_block.shape[1])
    zero_rows = jnp.zeros((row_count, feature_count), jnp.bfloat16)
    zero_stash = jnp.zeros((micro_count, row_count, feature_count), jnp.bfloat16)
    tick_count = sections + micro_count - 1

    def forward_tick(moment, state_now):
        incoming, stashed = state_now
        slot_index = moment - position
        is_live = (slot_index >= 0) & (slot_index < micro_count)
        position_in = jnp.clip(slot_index, 0, micro_count - 1)
        entering = lax.dynamic_index_in_dim(order, position_in, 0, keepdims=False)
        fed_row = lax.dynamic_index_in_dim(whole_inputs, entering, 0, keepdims=False)
        source_rows = jnp.where(position == 0, fed_row, incoming)
        result_rows = lax.cond(
            is_live,
            lambda: layer_forward(source_rows, first_block, second_block, gain_row, tables),
            lambda: zero_rows,
        )
        stashed = keep_slot(stashed, source_rows, position_in, is_live)
        incoming = shifted(result_rows, "section", 1)
        return (incoming, stashed)

    def backward_tick(moment, state_now, stashed):
        incoming, grads_out, grads_pre, normed_keep, mixed_keep = state_now
        slot_index = moment - (sections - 1 - position)
        is_live = (slot_index >= 0) & (slot_index < micro_count)
        position_in = jnp.clip(slot_index, 0, micro_count - 1)
        given_row = lax.dynamic_index_in_dim(whole_cotangent, position_in, 0, keepdims=False)
        arriving = jnp.where(position == sections - 1, given_row, incoming)
        hidden_in = lax.dynamic_index_in_dim(stashed, position_in, 0, keepdims=False)
        grad_in, grad_pre, normed, mixed = lax.cond(
            is_live,
            lambda: layer_backward(
                hidden_in, arriving, first_block, second_block, gain_row, tables
            ),
            lambda: (zero_rows, zero_rows, zero_rows, zero_rows),
        )
        grads_out = keep_slot(grads_out, arriving, position_in, is_live)
        grads_pre = keep_slot(grads_pre, grad_pre, position_in, is_live)
        normed_keep = keep_slot(normed_keep, normed, position_in, is_live)
        mixed_keep = keep_slot(mixed_keep, mixed, position_in, is_live)
        incoming = shifted(grad_in, "section", -1)
        return (incoming, grads_out, grads_pre, normed_keep, mixed_keep)

    start_forward = (zero_rows, zero_stash)
    start_backward = (zero_rows, zero_stash, zero_stash, zero_stash, zero_stash)
    forward = lax.fori_loop(0, tick_count, forward_tick, start_forward)
    stashed = forward[1]
    backward = lax.fori_loop(
        0,
        tick_count,
        lambda moment, state_now: backward_tick(moment, state_now, stashed),
        start_backward,
    )
    blocks = first_block.shape[0]
    block_size = first_block.shape[1]
    grads_out = backward[1].reshape(-1, blocks, block_size)
    grads_pre = backward[2].reshape(-1, blocks, block_size)
    normed_all = backward[3].reshape(-1, blocks, block_size)
    mixed_all = backward[4].reshape(-1, blocks, block_size)
    part_first = jnp.einsum(
        "tbi,tbj->bij", normed_all, grads_pre, preferred_element_type=jnp.float32
    )
    part_second = jnp.einsum(
        "tbi,tbj->bij", mixed_all, grads_out, preferred_element_type=jnp.float32
    )
    summed_first, summed_second = (
        lax.psum(part_first.astype(jnp.bfloat16), "dp").astype(jnp.float32),
        lax.psum(part_second.astype(jnp.bfloat16), "dp").astype(jnp.float32),
    )
    total_first = summed_first.astype(jnp.bfloat16)
    total_second = summed_second.astype(jnp.bfloat16)
    return (total_first[None], total_second[None])


MESH = pl.DeviceIdType.MESH
NT = (((1,), (1,)), ((), ()))
TN = (((0,), (0,)), ((), ()))


def rows_of(b):
    return pl.ds(pl.multiple_of(b * 128, 128), 128)


def step_kernel(
    S, NZ, NB, z0, cot, w1own, w2own, gown,
    out,
    w1, w2, grow, gcol, z, pre, act, fstage, mixed, bstage, brecv, gbuf, gpbuf, wbuf,
    ssend, srecv, rbuf, gsend, arecv, bsum, zrecv, csum, gath,
    wsend, wrecv, fsend, frecv, bsend, brsem, sssem, srsem,
    asend, arsem, zsend, zrsem, csend, crsem, dsend, drsem, esend, ersem, osem,
):
    me = lax.axis_index("section")
    at = lax.axis_index("dp")
    mz, my = at // 2, lax.rem(at, 2)
    half = NB // 2
    per = half // NZ
    AC = 128 // S
    D = S * NB * 128

    def peer(d):
        return lax.rem(me + d, S)

    def z_at(d):
        return lax.rem(mz + d, NZ)

    def z_peer(d):
        return {"dp": z_at(d) * 2 + my}

    def remote_to(src, dst, send, recv, device):
        return pltpu.make_async_remote_copy(
            src_ref=src, dst_ref=dst, send_sem=send, recv_sem=recv,
            device_id=device, device_id_type=MESH,
        )

    def remote(src, dst, send, recv, d):
        return remote_to(src, dst, send, recv, {"section": peer(d)})

    barrier = pltpu.get_barrier_semaphore()
    for d in range(1, S):
        pl.semaphore_signal(barrier, inc=1, device_id={"section": peer(d)}, device_id_type=MESH)
    y_peer = {"dp": mz * 2 + 1 - my}
    pl.semaphore_signal(barrier, inc=1, device_id=y_peer, device_id_type=MESH)
    for d in range(1, NZ):
        pl.semaphore_signal(barrier, inc=1, device_id=z_peer(d), device_id_type=MESH)
    pl.semaphore_wait(barrier, S + NZ - 1)

    own = ((gown, grow), (w1own, w1), (w2own, w2))

    def weight_copy(k, d):
        src, dst = own[k]
        part = src.at[pl.ds(peer(d) * NB, NB)]
        return remote(part, dst.at[me], wsend.at[k, d - 1], wrecv.at[k, me], d)

    def weight_local(k):
        src, dst = own[k]
        return pltpu.make_async_copy(src.at[pl.ds(me * NB, NB)], dst.at[me], wrecv.at[k, me])

    def weight_wait(k, l):
        src, dst = own[k]
        pltpu.make_async_copy(src.at[pl.ds(0, NB)], dst.at[l], wrecv.at[k, l]).wait()

    even = lax.rem(me, 2) == 0
    for k in range(3):
        weight_local(k).start()
    for d in range(1, S):
        weight_copy(0, d).start()

    @pl.when(even)
    def _():
        for d in range(1, S):
            weight_copy(1, d).start()

    def sums_copy(k, d):
        return remote(ssend.at[k], srecv.at[k, d - 1], sssem.at[k, d - 1], srsem.at[k, d - 1], d)

    def sums_start(k, value):
        ssend[k] = jnp.broadcast_to(value, (8, 128))
        for d in range(1, S):
            sums_copy(k, d).start()

    def sums_wait(k):
        for d in range(1, S):
            sums_copy(k, d).wait()
        total = ssend[k]
        for d in range(1, S):
            total = total + srecv[k, d - 1]
        return total[0:1, :]

    def fcopy(l, d):
        return remote(
            fstage.at[l, pl.ds(peer(d) * AC, AC)], mixed.at[l, me],
            fsend.at[l, d - 1], frecv.at[l, d - 1], d,
        )

    def bcopy(l, d):
        return remote(
            bstage.at[l, peer(d)], brecv.at[l, pl.ds(me * AC, AC)],
            bsend.at[l, d - 1], brsem.at[l, d - 1], d,
        )

    def mixed_block(l, b):
        parts = [mixed[l, :, 2 * b + p].reshape(S * NB, 128) for p in range(2)]
        return jnp.concatenate(parts, axis=0)

    def back_send(l):
        def block(b, carry):
            gm = jnp.dot(w2[l, b], gbuf[rows_of(b)], preferred_element_type=jnp.float32)
            gm = gm.astype(jnp.bfloat16)
            for p in range(2):
                for s in range(S):
                    at = (p * S + s) * NB
                    bstage[l, s, 2 * b + p] = gm[at:at + NB]
            return carry
        lax.fori_loop(0, NB, block, 0, unroll=UNROLL)
        for d in range(1, S):
            bcopy(l, d).start()
        brecv[l, pl.ds(me * AC, AC)] = bstage[l, me]

    def squares(b, total):
        zb = z[0, rows_of(b)].astype(jnp.float32)
        return total + jnp.sum(zb * zb, axis=0, keepdims=True)

    zero = jnp.zeros((1, 128), jnp.float32)

    def load_z(b, carry):
        z[0, rows_of(b)] = z0[rows_of(b)]
        gbuf[rows_of(b)] = cot[rows_of(b)]
        return carry
    lax.fori_loop(0, NB, load_z, 0)
    sums_start(0, lax.fori_loop(0, NB, squares, zero))

    for l in range(S):
        weight_wait(0, l)

    def spread(q, carry):
        l = q // NB
        b = lax.rem(q, NB)
        line = jnp.broadcast_to(grow[l, pl.ds(b, 1)], (128, 128))
        gcol[l, rows_of(b)] = line.T
        return carry
    lax.fori_loop(0, S * NB, spread, 0)

    def forward(l, last):
        if not last:
            @pl.when((l == 0) & even)
            def _():
                for d in range(1, S):
                    weight_copy(1, d).wait_send()
                for d in range(2, S):
                    weight_copy(2, d).start()

            @pl.when((l == 1) & jnp.logical_not(even))
            def _():
                for d in range(1, S):
                    weight_copy(1, d).wait_send()
                for d in range(1, S):
                    weight_copy(2, d).start()
        weight_wait(1, l)

        def first(b, carry):
            zg = (z[l, rows_of(b)].astype(jnp.float32) * gcol[l, rows_of(b)]).astype(jnp.bfloat16)
            pre[l, rows_of(b)] = lax.dot_general(
                w1[l, b], zg, TN, preferred_element_type=jnp.float32
            )
            return carry
        lax.fori_loop(0, NB, first, 0, unroll=UNROLL)
        r = lax.rsqrt(sums_wait(l) * (1.0 / D) + EPS)
        rbuf[l] = jnp.broadcast_to(r, (8, 128))

        def gate(b, carry):
            value = pre[l, rows_of(b)] * r
            pre[l, rows_of(b)] = value
            act[rows_of(b)] = value * jax.nn.sigmoid(value)
            return carry
        lax.fori_loop(0, NB, gate, 0, unroll=UNROLL)

        def pack(a, carry):
            fstage[l, a] = act[pl.ds(a, NB, stride=128), :].astype(jnp.bfloat16)
            return carry
        lax.fori_loop(0, 128, pack, 0, unroll=8)
        for d in range(1, S):
            fcopy(l, d).start()
        mixed[l, me] = fstage[l, pl.ds(me * AC, AC)]
        if not last:
            @pl.when((l == 0) & even)
            def _():
                for d in range(2, S):
                    weight_copy(2, d).wait_send()
                weight_copy(2, 1).start()
        weight_wait(2, l)
        if not last:
            @pl.when((l == 0) & jnp.logical_not(even))
            def _():
                for d in range(1, S):
                    weight_copy(1, d).start()
        if last:
            back_send(l)
            for d in range(1, S):
                fcopy(l, d).wait()
            return
        for d in range(1, S):
            fcopy(l, d).wait()

        def second(b, total):
            out = lax.dot_general(
                w2[l, b], mixed_block(l, b), TN, preferred_element_type=jnp.float32
            )
            zn = (z[l, rows_of(b)].astype(jnp.float32) + out).astype(jnp.bfloat16)
            z[l + 1, rows_of(b)] = zn
            zf = zn.astype(jnp.float32)
            return total + jnp.sum(zf * zf, axis=0, keepdims=True)
        sums_start(l + 1, lax.fori_loop(0, NB, second, zero, unroll=UNROLL))

    def a_copy(l, f):
        return remote_to(
            gsend.at[l, f, 1 - my], arecv.at[l, f], asend.at[l, f], arsem.at[l, f], y_peer
        )

    def b_copy(l, f, d):
        return remote_to(
            bsum.at[l, f, pl.ds(z_at(d) * per, per)], zrecv.at[l, f, d - 1],
            zsend.at[l, f, d - 1], zrsem.at[l, f, d - 1], z_peer(d),
        )

    def c_copy(l, f):
        return remote_to(
            csum.at[l, f], gath.at[f, me, my, mz], csend.at[l, f], crsem.at[f, me], {"section": l}
        )

    def d_copy(f, d):
        part = gath.at[f, :, my, mz]
        return remote_to(part, part, dsend.at[f, d - 1], drsem.at[f, d - 1], z_peer(d))

    def e_copy(f, d):
        part = gath.at[f, :, my, lax.rem(mz + NZ - d, NZ)]
        return remote_to(part, part, esend.at[f, d], ersem.at[f, d], y_peer)

    def stage_b(l, f):
        a_copy(l, f).wait_recv()

        def tile(i, carry):
            total = gsend[l, f, my, i].astype(jnp.float32) + arecv[l, f, i].astype(jnp.float32)
            bsum[l, f, i] = total.astype(jnp.bfloat16)
            return carry
        lax.fori_loop(0, half, tile, 0)
        for d in range(1, NZ):
            b_copy(l, f, d).start()

    def stage_c(l, f):
        for d in range(1, NZ):
            b_copy(l, f, d).wait_recv()
        for i in range(per):
            total = bsum[l, f, mz * per + i].astype(jnp.float32)
            for d in range(1, NZ):
                total = total + zrecv[l, f, d - 1, i].astype(jnp.float32)
            csum[l, f, i] = total.astype(jnp.bfloat16)

        @pl.when(me == l)
        def _():
            gath[f, me, my, mz] = csum[l, f]

        @pl.when(me != l)
        def _():
            c_copy(l, f).start()

    def stage_d(l, f):
        @pl.when(me == l)
        def _():
            for d in range(1, S):
                part = gath.at[f, peer(d), my, mz]
                pltpu.make_async_copy(csum.at[l, f], part, crsem.at[f, peer(d)]).wait()
            for d in range(1, NZ):
                d_copy(f, d).start()
            e_copy(f, 0).start()

    def stage_e(l, f):
        @pl.when(me == l)
        def _():
            for d in range(1, NZ):
                d_copy(f, d).wait_recv()
                e_copy(f, d).start()

    def both(stage, l):
        for f in (1, 0):
            stage(l, f)

    def backward(l, last):
        def grad_second(b, carry):
            gsend[l, 1, b // half, lax.rem(b, half)] = lax.dot_general(
                mixed_block(l, b), gbuf[rows_of(b)], NT, preferred_element_type=jnp.float32
            ).astype(jnp.bfloat16)
            return carry
        lax.fori_loop(0, NB, grad_second, 0, unroll=UNROLL)
        a_copy(l, 1).start()

        @pl.when(l < S - 1)
        def _():
            stage_b(l + 1, 0)

        @pl.when(l < S - 2)
        def _():
            stage_c(l + 2, 0)
            stage_d(l + 2, 1)
        for d in range(1, S):
            bcopy(l, d).wait()

        def unpack(a, carry):
            act[pl.ds(a, NB, stride=128), :] = brecv[l, a].astype(jnp.float32)
            return carry
        lax.fori_loop(0, 128, unpack, 0, unroll=8)
        r = rbuf[l][0:1, :]

        def gate(b, total):
            value = pre[l, rows_of(b)]
            s = jax.nn.sigmoid(value)
            gp = (act[rows_of(b)] * s * (1.0 + value * (1.0 - s))).astype(jnp.bfloat16)
            gpbuf[rows_of(b)] = gp
            if last:
                return total
            w = jnp.dot(w1[l, b], gp, preferred_element_type=jnp.float32) * gcol[l, rows_of(b)]
            wbuf[rows_of(b)] = w
            u = z[l, rows_of(b)].astype(jnp.float32) * r
            return total + jnp.sum(w * u, axis=0, keepdims=True)
        total = lax.fori_loop(0, NB, gate, zero, unroll=UNROLL)
        if not last:
            sums_start(S + l, total)

        def grad_first(b, carry):
            u = z[l, rows_of(b)].astype(jnp.float32) * r
            normed = (u * gcol[l, rows_of(b)]).astype(jnp.bfloat16)
            gsend[l, 0, b // half, lax.rem(b, half)] = lax.dot_general(
                normed, gpbuf[rows_of(b)], NT, preferred_element_type=jnp.float32
            ).astype(jnp.bfloat16)
            return carry
        lax.fori_loop(0, NB, grad_first, 0, unroll=UNROLL)
        a_copy(l, 0).start()

        stage_b(l, 1)

        @pl.when(l < S - 1)
        def _():
            stage_c(l + 1, 1)

        @pl.when(l < S - 2)
        def _():
            stage_d(l + 2, 0)
        if last:
            return
        c = sums_wait(S + l) * (1.0 / D)

        def grad_in(b, carry):
            u = z[l, rows_of(b)].astype(jnp.float32) * r
            gf = gbuf[rows_of(b)].astype(jnp.float32) + r * (wbuf[rows_of(b)] - u * c)
            gbuf[rows_of(b)] = gf.astype(jnp.bfloat16)
            return carry
        lax.fori_loop(0, NB, grad_in, 0, unroll=UNROLL)

    def forward_step(l, carry):
        forward(l, False)
        return carry
    lax.fori_loop(0, S - 1, forward_step, 0)
    forward(S - 1, True)

    def backward_step(k, carry):
        l = S - 1 - k
        backward(l, False)
        back_send(l - 1)
        return carry
    lax.fori_loop(0, S - 1, backward_step, 0)
    backward(0, True)
    stage_d(1, 1)
    stage_b(0, 0)
    stage_c(1, 0)
    stage_c(0, 1)
    for l in range(S - 1, 1, -1):
        both(stage_e, l)
    stage_e(1, 1)
    stage_d(1, 0)
    stage_c(0, 0)
    stage_d(0, 1)
    stage_e(1, 0)
    stage_e(0, 1)
    stage_d(0, 0)
    stage_e(0, 0)
    for f in range(2):
        for d in range(NZ):
            e_copy(f, d).wait_recv()
    done = pltpu.make_async_copy(gath, out, osem.at[0])
    done.start()

    def finish(l, carry):
        for f in range(2):
            a_copy(l, f).wait_send()
            for d in range(1, NZ):
                b_copy(l, f, d).wait_send()

            @pl.when(me != l)
            def _():
                c_copy(l, f).wait_send()
        return carry
    lax.fori_loop(0, S, finish, 0)
    for f in range(2):
        for d in range(1, NZ):
            d_copy(f, d).wait_send()
        for d in range(NZ):
            e_copy(f, d).wait_send()
    done.wait()

    for d in range(1, S):
        weight_copy(0, d).wait_send()
    weight_copy(2, 1).wait_send()

    @pl.when(jnp.logical_not(even))
    def _():
        for d in range(2, S):
            weight_copy(2, d).wait_send()


UNROLL = 4


def local_step(S, NZ, NB, z0, cot, w1own, w2own, gown):
    F = NB * 128
    AC = 128 // S
    bf, f32 = jnp.bfloat16, jnp.float32
    vmem = pl.BlockSpec(memory_space=pltpu.VMEM)
    dma = pltpu.SemaphoreType.DMA
    half = NB // 2
    per = half // NZ
    shape = jax.ShapeDtypeStruct((2, S, 2, NZ, per, 128, 128), bf)
    return pl.pallas_call(
        functools.partial(step_kernel, S, NZ, NB),
        out_shape=shape,
        in_specs=[vmem] * 5,
        out_specs=pl.BlockSpec(memory_space=pl.ANY),
        scratch_shapes=[
            pltpu.VMEM((S, NB, 128, 128), bf),
            pltpu.VMEM((S, NB, 128, 128), bf),
            pltpu.VMEM((S, NB, 128), f32),
            pltpu.VMEM((S, F, 128), f32),
            pltpu.VMEM((S, F, 128), bf),
            pltpu.VMEM((S, F, 128), f32),
            pltpu.VMEM((F, 128), f32),
            pltpu.VMEM((S, 128, NB, 128), bf),
            pltpu.VMEM((S, S, AC, NB, 128), bf),
            pltpu.VMEM((S, S, AC, NB, 128), bf),
            pltpu.VMEM((S, 128, NB, 128), bf),
            pltpu.VMEM((F, 128), bf),
            pltpu.VMEM((F, 128), bf),
            pltpu.VMEM((F, 128), f32),
            pltpu.VMEM((2 * S, 8, 128), f32),
            pltpu.VMEM((2 * S, S - 1, 8, 128), f32),
            pltpu.VMEM((S, 8, 128), f32),
            pltpu.VMEM((S, 2, 2, half, 128, 128), bf),
            pltpu.VMEM((S, 2, half, 128, 128), bf),
            pltpu.VMEM((S, 2, half, 128, 128), bf),
            pltpu.VMEM((S, 2, NZ - 1, per, 128, 128), bf),
            pltpu.VMEM((S, 2, per, 128, 128), bf),
            pltpu.VMEM((2, S, 2, NZ, per, 128, 128), bf),
            dma((3, S - 1)),
            dma((3, S)),
            dma((S, S - 1)),
            dma((S, S - 1)),
            dma((S, S - 1)),
            dma((S, S - 1)),
            dma((2 * S, S - 1)),
            dma((2 * S, S - 1)),
            dma((S, 2)),
            dma((S, 2)),
            dma((S, 2, NZ - 1)),
            dma((S, 2, NZ - 1)),
            dma((S, 2)),
            dma((2, S)),
            dma((2, NZ - 1)),
            dma((2, NZ - 1)),
            dma((2, NZ)),
            dma((2, NZ)),
            dma((1,)),
        ],
        compiler_params=pltpu.CompilerParams(
            collective_id=0, has_side_effects=True, vmem_limit_bytes=58 * 1024 * 1024
        ),
        name="step",
    )(z0, cot, w1own, w2own, gown)


def fast_body(inputs, cotangent, first_factor, second_factor, gains, mixing, order):
    sections = lax.axis_size("section")
    first_block, second_block = first_factor[0], second_factor[0]
    blocks, size = first_block.shape[0], first_block.shape[1]
    NB = blocks // sections
    block_table, lane_table = mixing_tables(mixing[0], blocks, size)
    w1p = jnp.einsum(
        "bij,ja->bia", first_block, lane_table, preferred_element_type=jnp.float32
    ).astype(jnp.bfloat16)
    w2p = jnp.einsum(
        "be,qpej->qpbj", block_table, second_block.reshape(blocks, 2, blocks, size),
        preferred_element_type=jnp.float32,
    ).astype(jnp.bfloat16).reshape(blocks, size, size)
    rows = inputs.shape[0] * inputs.shape[1]
    z0 = jnp.take(inputs, order, axis=0).reshape(rows, -1).T
    cot = cotangent.reshape(rows, -1).T
    total = local_step(
        sections, lax.axis_size("dp") // 2, NB, z0, cot, w1p, w2p, gains[0].reshape(blocks, size)
    )
    t1 = total[0].reshape(blocks, size, size)
    t2 = total[1].reshape(blocks, 2, blocks, size)
    out1 = jnp.einsum(
        "bia,ja->bij", t1, lane_table, preferred_element_type=jnp.float32
    ).astype(jnp.bfloat16)
    out2 = jnp.einsum(
        "be,qpbj->qpej", block_table, t2, preferred_element_type=jnp.float32
    ).astype(jnp.bfloat16).reshape(blocks, size, size)
    return (out1[None], out2[None])


def solution(mesh):
    quick = mesh.shape["section"] == 4 and mesh.shape["dp"] == 8
    return jax.shard_map(
        fast_body if quick else body,
        mesh=mesh,
        in_specs=(
            P(None, "dp", "section"),
            P(None, "dp", "section"),
            P("section", None, None, None),
            P("section", None, None, None),
            P("section", None),
            P("section", None),
            P(),
        ),
        out_specs=(P("section", None, None, None), P("section", None, None, None)),
        check_vma=False,
    )
```

```python
import functools

import jax
import jax.numpy as jnp
from jax import lax
from jax.experimental import pallas as pl
from jax.experimental.pallas import tpu as pltpu
from jax.sharding import PartitionSpec as P

EPS = 1e-05


def shifted(x, axis, by):
    devices = lax.axis_size(axis)
    pairs = [(i, i + by) for i in range(devices) if 0 <= i + by < devices]
    return lax.ppermute(x, axis, pairs)


def block_apply(values, factor):
    row_count = values.shape[0]
    shaped = values.reshape(row_count, factor.shape[0], factor.shape[1])
    return jnp.einsum("tbi,bij->tbj", shaped, factor, preferred_element_type=jnp.float32).reshape(
        row_count, -1
    )


def block_apply_back(values, factor):
    row_count = values.shape[0]
    shaped = values.reshape(row_count, factor.shape[0], factor.shape[1])
    return jnp.einsum("tbj,bij->tbi", shaped, factor, preferred_element_type=jnp.float32).reshape(
        row_count, -1
    )


def mixing_tables(mixing_row, blocks, block_size):
    block_ids = mixing_row[:blocks] // block_size
    lane_ids = mixing_row[::blocks] % block_size
    block_table = (jnp.arange(blocks, dtype=jnp.int32)[:, None] == block_ids[None, :]).astype(
        jnp.bfloat16
    )
    lane_table = (jnp.arange(block_size, dtype=jnp.int32)[:, None] == lane_ids[None, :]).astype(
        jnp.bfloat16
    )
    return (block_table, lane_table)


def mix_forward(active, tables):
    block_table, lane_table = tables
    row_count = active.shape[0]
    shaped = active.reshape(row_count, block_table.shape[0], lane_table.shape[0])
    halfway = jnp.einsum(
        "tbi,ia->tba", shaped, lane_table, preferred_element_type=jnp.float32
    ).astype(jnp.bfloat16)
    moved = jnp.einsum(
        "tba,be->tae", halfway, block_table, preferred_element_type=jnp.float32
    ).astype(jnp.bfloat16)
    return moved.reshape(row_count, -1)


def mix_backward(grad_mixed, tables):
    block_table, lane_table = tables
    row_count = grad_mixed.shape[0]
    shaped = grad_mixed.reshape(row_count, lane_table.shape[0], block_table.shape[0])
    halfway = jnp.einsum(
        "tae,be->tab", shaped, block_table, preferred_element_type=jnp.float32
    ).astype(jnp.bfloat16)
    moved = jnp.einsum(
        "tab,ia->tbi", halfway, lane_table, preferred_element_type=jnp.float32
    ).astype(jnp.bfloat16)
    return moved.reshape(row_count, -1)


def branch_forward(hidden_in, first_block, gain_row, tables):
    as_float = hidden_in.astype(jnp.float32)
    scale_inv = lax.rsqrt(jnp.mean(as_float * as_float, axis=-1, keepdims=True) + EPS)
    unit_rows = as_float * scale_inv
    normed = (unit_rows * gain_row).astype(jnp.bfloat16)
    pre_act = block_apply(normed, first_block)
    active = (pre_act * jax.nn.sigmoid(pre_act)).astype(jnp.bfloat16)
    mixed = mix_forward(active, tables)
    return (normed, unit_rows, scale_inv, pre_act, mixed)


def layer_forward(hidden_in, first_block, second_block, gain_row, tables):
    pieces = branch_forward(hidden_in, first_block, gain_row, tables)
    return (hidden_in.astype(jnp.float32) + block_apply(pieces[4], second_block)).astype(
        jnp.bfloat16
    )


def layer_backward(hidden_in, grad_out, first_block, second_block, gain_row, tables):
    normed, unit_rows, scale_inv, pre_act, mixed = branch_forward(
        hidden_in, first_block, gain_row, tables
    )
    grad_mixed = block_apply_back(grad_out, second_block).astype(jnp.bfloat16)
    grad_active = mix_backward(grad_mixed, tables)
    gate_sig = jax.nn.sigmoid(pre_act)
    grad_pre = (
        grad_active.astype(jnp.float32) * gate_sig * (1.0 + pre_act * (1.0 - gate_sig))
    ).astype(jnp.bfloat16)
    grad_normed = block_apply_back(grad_pre, first_block)
    grad_unit = grad_normed * gain_row
    correction = jnp.mean(grad_unit * unit_rows, axis=-1, keepdims=True)
    grad_in = (
        grad_out.astype(jnp.float32) + scale_inv * (grad_unit - unit_rows * correction)
    ).astype(jnp.bfloat16)
    return (grad_in, grad_pre, normed, mixed)


def keep_slot(buffer, value, slot, is_live):
    previous = lax.dynamic_index_in_dim(buffer, slot, 0, keepdims=False)
    return lax.dynamic_update_index_in_dim(buffer, jnp.where(is_live, value, previous), slot, 0)


def body(inputs, cotangent, first_factor, second_factor, gains, mixing, order):
    sections = lax.axis_size("section")
    position = lax.axis_index("section")
    micro_count = inputs.shape[0]
    row_count = inputs.shape[1]
    whole_inputs, whole_cotangent = (
        lax.all_gather(inputs, "section", axis=2, tiled=True),
        lax.all_gather(cotangent, "section", axis=2, tiled=True),
    )
    feature_count = whole_inputs.shape[2]
    first_block = first_factor[0]
    second_block = second_factor[0]
    gain_row = gains[0]
    tables = mixing_tables(mixing[0], first_block.shape[0], first_block.shape[1])
    zero_rows = jnp.zeros((row_count, feature_count), jnp.bfloat16)
    zero_stash = jnp.zeros((micro_count, row_count, feature_count), jnp.bfloat16)
    tick_count = sections + micro_count - 1

    def forward_tick(moment, state_now):
        incoming, stashed = state_now
        slot_index = moment - position
        is_live = (slot_index >= 0) & (slot_index < micro_count)
        position_in = jnp.clip(slot_index, 0, micro_count - 1)
        entering = lax.dynamic_index_in_dim(order, position_in, 0, keepdims=False)
        fed_row = lax.dynamic_index_in_dim(whole_inputs, entering, 0, keepdims=False)
        source_rows = jnp.where(position == 0, fed_row, incoming)
        result_rows = lax.cond(
            is_live,
            lambda: layer_forward(source_rows, first_block, second_block, gain_row, tables),
            lambda: zero_rows,
        )
        stashed = keep_slot(stashed, source_rows, position_in, is_live)
        incoming = shifted(result_rows, "section", 1)
        return (incoming, stashed)

    def backward_tick(moment, state_now, stashed):
        incoming, grads_out, grads_pre, normed_keep, mixed_keep = state_now
        slot_index = moment - (sections - 1 - position)
        is_live = (slot_index >= 0) & (slot_index < micro_count)
        position_in = jnp.clip(slot_index, 0, micro_count - 1)
        given_row = lax.dynamic_index_in_dim(whole_cotangent, position_in, 0, keepdims=False)
        arriving = jnp.where(position == sections - 1, given_row, incoming)
        hidden_in = lax.dynamic_index_in_dim(stashed, position_in, 0, keepdims=False)
        grad_in, grad_pre, normed, mixed = lax.cond(
            is_live,
            lambda: layer_backward(
                hidden_in, arriving, first_block, second_block, gain_row, tables
            ),
            lambda: (zero_rows, zero_rows, zero_rows, zero_rows),
        )
        grads_out = keep_slot(grads_out, arriving, position_in, is_live)
        grads_pre = keep_slot(grads_pre, grad_pre, position_in, is_live)
        normed_keep = keep_slot(normed_keep, normed, position_in, is_live)
        mixed_keep = keep_slot(mixed_keep, mixed, position_in, is_live)
        incoming = shifted(grad_in, "section", -1)
        return (incoming, grads_out, grads_pre, normed_keep, mixed_keep)

    start_forward = (zero_rows, zero_stash)
    start_backward = (zero_rows, zero_stash, zero_stash, zero_stash, zero_stash)
    forward = lax.fori_loop(0, tick_count, forward_tick, start_forward)
    stashed = forward[1]
    backward = lax.fori_loop(
        0,
        tick_count,
        lambda moment, state_now: backward_tick(moment, state_now, stashed),
        start_backward,
    )
    blocks = first_block.shape[0]
    block_size = first_block.shape[1]
    grads_out = backward[1].reshape(-1, blocks, block_size)
    grads_pre = backward[2].reshape(-1, blocks, block_size)
    normed_all = backward[3].reshape(-1, blocks, block_size)
    mixed_all = backward[4].reshape(-1, blocks, block_size)
    part_first = jnp.einsum(
        "tbi,tbj->bij", normed_all, grads_pre, preferred_element_type=jnp.float32
    )
    part_second = jnp.einsum(
        "tbi,tbj->bij", mixed_all, grads_out, preferred_element_type=jnp.float32
    )
    summed_first, summed_second = (
        lax.psum(part_first.astype(jnp.bfloat16), "dp").astype(jnp.float32),
        lax.psum(part_second.astype(jnp.bfloat16), "dp").astype(jnp.float32),
    )
    total_first = summed_first.astype(jnp.bfloat16)
    total_second = summed_second.astype(jnp.bfloat16)
    return (total_first[None], total_second[None])


MESH = pl.DeviceIdType.MESH
NT = (((1,), (1,)), ((), ()))
TN = (((0,), (0,)), ((), ()))


def rows_of(b):
    return pl.ds(pl.multiple_of(b * 128, 128), 128)


def step_kernel(
    S, NZ, NB, z0, cot, w1own, w2own, gown,
    out,
    w1, w2, grow, gcol, z, pre, act, fstage, mixed, bstage, brecv, gbuf, gpbuf, wbuf,
    ssend, srecv, rbuf, gsend, arecv, bsum, zrecv, csum, gath,
    wsend, wrecv, fsend, frecv, bsend, brsem, sssem, srsem,
    asend, arsem, zsend, zrsem, csend, crsem, dsend, drsem, esend, ersem, osem,
):
    me = lax.axis_index("section")
    at = lax.axis_index("dp")
    mz, my = at // 2, lax.rem(at, 2)
    half = NB // 2
    per = half // NZ
    AC = 128 // S
    D = S * NB * 128

    def peer(d):
        return lax.rem(me + d, S)

    def z_at(d):
        return lax.rem(mz + d, NZ)

    def z_peer(d):
        return {"dp": z_at(d) * 2 + my}

    def remote_to(src, dst, send, recv, device):
        return pltpu.make_async_remote_copy(
            src_ref=src, dst_ref=dst, send_sem=send, recv_sem=recv,
            device_id=device, device_id_type=MESH,
        )

    def remote(src, dst, send, recv, d):
        return remote_to(src, dst, send, recv, {"section": peer(d)})

    barrier = pltpu.get_barrier_semaphore()
    for d in range(1, S):
        pl.semaphore_signal(barrier, inc=1, device_id={"section": peer(d)}, device_id_type=MESH)
    y_peer = {"dp": mz * 2 + 1 - my}
    pl.semaphore_signal(barrier, inc=1, device_id=y_peer, device_id_type=MESH)
    for d in range(1, NZ):
        pl.semaphore_signal(barrier, inc=1, device_id=z_peer(d), device_id_type=MESH)
    pl.semaphore_wait(barrier, S + NZ - 1)

    own = ((gown, grow), (w1own, w1), (w2own, w2))

    def weight_copy(k, d):
        src, dst = own[k]
        part = src.at[pl.ds(peer(d) * NB, NB)]
        return remote(part, dst.at[me], wsend.at[k, d - 1], wrecv.at[k, me], d)

    def weight_local(k):
        src, dst = own[k]
        return pltpu.make_async_copy(src.at[pl.ds(me * NB, NB)], dst.at[me], wrecv.at[k, me])

    def weight_wait(k, l):
        src, dst = own[k]
        pltpu.make_async_copy(src.at[pl.ds(0, NB)], dst.at[l], wrecv.at[k, l]).wait()

    even = lax.rem(me, 2) == 0
    for k in range(3):
        weight_local(k).start()
    for d in range(1, S):
        weight_copy(0, d).start()

    @pl.when(even)
    def _():
        for d in range(1, S):
            weight_copy(1, d).start()

    def sums_copy(k, d):
        return remote(ssend.at[k], srecv.at[k, d - 1], sssem.at[k, d - 1], srsem.at[k, d - 1], d)

    def sums_start(k, value):
        ssend[k] = jnp.broadcast_to(value, (8, 128))
        for d in range(1, S):
            sums_copy(k, d).start()

    def sums_wait(k):
        for d in range(1, S):
            sums_copy(k, d).wait()
        total = ssend[k]
        for d in range(1, S):
            total = total + srecv[k, d - 1]
        return total[0:1, :]

    def fcopy(l, d):
        return remote(
            fstage.at[l, pl.ds(peer(d) * AC, AC)], mixed.at[l, me],
            fsend.at[l, d - 1], frecv.at[l, d - 1], d,
        )

    def bcopy(l, d):
        return remote(
            bstage.at[l, peer(d)], brecv.at[l, pl.ds(me * AC, AC)],
            bsend.at[l, d - 1], brsem.at[l, d - 1], d,
        )

    def mixed_block(l, b):
        parts = [mixed[l, :, 2 * b + p].reshape(S * NB, 128) for p in range(2)]
        return jnp.concatenate(parts, axis=0)

    def back_send(l):
        def block(b, carry):
            gm = jnp.dot(w2[l, b], gbuf[rows_of(b)], preferred_element_type=jnp.float32)
            gm = gm.astype(jnp.bfloat16)
            for p in range(2):
                for s in range(S):
                    at = (p * S + s) * NB
                    bstage[l, s, 2 * b + p] = gm[at:at + NB]
            return carry
        lax.fori_loop(0, NB, block, 0, unroll=UNROLL)
        for d in range(1, S):
            bcopy(l, d).start()
        brecv[l, pl.ds(me * AC, AC)] = bstage[l, me]

    def squares(b, total):
        zb = z[0, rows_of(b)].astype(jnp.float32)
        return total + jnp.sum(zb * zb, axis=0, keepdims=True)

    zero = jnp.zeros((1, 128), jnp.float32)

    def load_z(b, carry):
        z[0, rows_of(b)] = z0[rows_of(b)]
        gbuf[rows_of(b)] = cot[rows_of(b)]
        return carry
    lax.fori_loop(0, NB, load_z, 0)
    sums_start(0, lax.fori_loop(0, NB, squares, zero))

    for l in range(S):
        weight_wait(0, l)

    def spread(q, carry):
        l = q // NB
        b = lax.rem(q, NB)
        line = jnp.broadcast_to(grow[l, pl.ds(b, 1)], (128, 128))
        gcol[l, rows_of(b)] = line.T
        return carry
    lax.fori_loop(0, S * NB, spread, 0)

    def forward(l, last):
        if not last:
            @pl.when((l == 0) & even)
            def _():
                for d in range(1, S):
                    weight_copy(1, d).wait_send()
                for d in range(2, S):
                    weight_copy(2, d).start()

            @pl.when((l == 1) & jnp.logical_not(even))
            def _():
                for d in range(1, S):
                    weight_copy(1, d).wait_send()
                for d in range(1, S):
                    weight_copy(2, d).start()
        weight_wait(1, l)

        def first(b, carry):
            zg = (z[l, rows_of(b)].astype(jnp.float32) * gcol[l, rows_of(b)]).astype(jnp.bfloat16)
            pre[l, rows_of(b)] = lax.dot_general(
                w1[l, b], zg, TN, preferred_element_type=jnp.float32
            )
            return carry
        lax.fori_loop(0, NB, first, 0, unroll=UNROLL)
        r = lax.rsqrt(sums_wait(l) * (1.0 / D) + EPS)
        rbuf[l] = jnp.broadcast_to(r, (8, 128))

        def gate(b, carry):
            value = pre[l, rows_of(b)] * r
            pre[l, rows_of(b)] = value
            act[rows_of(b)] = value * jax.nn.sigmoid(value)
            return carry
        lax.fori_loop(0, NB, gate, 0, unroll=UNROLL)

        def pack(a, carry):
            fstage[l, a] = act[pl.ds(a, NB, stride=128), :].astype(jnp.bfloat16)
            return carry
        lax.fori_loop(0, 128, pack, 0, unroll=8)
        for d in range(1, S):
            fcopy(l, d).start()
        mixed[l, me] = fstage[l, pl.ds(me * AC, AC)]
        if not last:
            @pl.when((l == 0) & even)
            def _():
                for d in range(2, S):
                    weight_copy(2, d).wait_send()
                weight_copy(2, 1).start()
        weight_wait(2, l)
        if not last:
            @pl.when((l == 0) & jnp.logical_not(even))
            def _():
                for d in range(1, S):
                    weight_copy(1, d).start()
        if last:
            back_send(l)
            for d in range(1, S):
                fcopy(l, d).wait()
            return
        for d in range(1, S):
            fcopy(l, d).wait()

        def second(b, total):
            out = lax.dot_general(
                w2[l, b], mixed_block(l, b), TN, preferred_element_type=jnp.float32
            )
            zn = (z[l, rows_of(b)].astype(jnp.float32) + out).astype(jnp.bfloat16)
            z[l + 1, rows_of(b)] = zn
            zf = zn.astype(jnp.float32)
            return total + jnp.sum(zf * zf, axis=0, keepdims=True)
        sums_start(l + 1, lax.fori_loop(0, NB, second, zero, unroll=UNROLL))

    def a_copy(l, f):
        return remote_to(
            gsend.at[l, f, 1 - my], arecv.at[l, f], asend.at[l, f], arsem.at[l, f], y_peer
        )

    def b_copy(l, f, d):
        return remote_to(
            bsum.at[l, f, pl.ds(z_at(d) * per, per)], zrecv.at[l, f, d - 1],
            zsend.at[l, f, d - 1], zrsem.at[l, f, d - 1], z_peer(d),
        )

    def c_copy(l, f):
        return remote_to(
            csum.at[l, f], gath.at[f, me, my, mz], csend.at[l, f], crsem.at[f, me], {"section": l}
        )

    def d_copy(f, d):
        part = gath.at[f, :, my, mz]
        return remote_to(part, part, dsend.at[f, d - 1], drsem.at[f, d - 1], z_peer(d))

    def e_copy(f, d):
        part = gath.at[f, :, my, lax.rem(mz + NZ - d, NZ)]
        return remote_to(part, part, esend.at[f, d], ersem.at[f, d], y_peer)

    def stage_b(l, f):
        a_copy(l, f).wait_recv()

        def tile(i, carry):
            total = gsend[l, f, my, i].astype(jnp.float32) + arecv[l, f, i].astype(jnp.float32)
            bsum[l, f, i] = total.astype(jnp.bfloat16)
            return carry
        lax.fori_loop(0, half, tile, 0)
        for d in range(1, NZ):
            b_copy(l, f, d).start()

    def stage_c(l, f):
        for d in range(1, NZ):
            b_copy(l, f, d).wait_recv()
        for i in range(per):
            total = bsum[l, f, mz * per + i].astype(jnp.float32)
            for d in range(1, NZ):
                total = total + zrecv[l, f, d - 1, i].astype(jnp.float32)
            csum[l, f, i] = total.astype(jnp.bfloat16)

        @pl.when(me == l)
        def _():
            gath[f, me, my, mz] = csum[l, f]

        @pl.when(me != l)
        def _():
            c_copy(l, f).start()

    def stage_d(l, f):
        @pl.when(me == l)
        def _():
            for d in range(1, S):
                part = gath.at[f, peer(d), my, mz]
                pltpu.make_async_copy(csum.at[l, f], part, crsem.at[f, peer(d)]).wait()
            for d in range(1, NZ):
                d_copy(f, d).start()
            e_copy(f, 0).start()

    def stage_e(l, f):
        @pl.when(me == l)
        def _():
            for d in range(1, NZ):
                d_copy(f, d).wait_recv()
                e_copy(f, d).start()

    def both(stage, l):
        for f in (1, 0):
            stage(l, f)

    def backward(l, last):
        def grad_second(b, carry):
            gsend[l, 1, b // half, lax.rem(b, half)] = lax.dot_general(
                mixed_block(l, b), gbuf[rows_of(b)], NT, preferred_element_type=jnp.float32
            ).astype(jnp.bfloat16)
            return carry
        lax.fori_loop(0, NB, grad_second, 0, unroll=UNROLL)
        a_copy(l, 1).start()

        @pl.when(l < S - 1)
        def _():
            stage_b(l + 1, 0)

        @pl.when(l < S - 2)
        def _():
            stage_c(l + 2, 0)
            stage_d(l + 2, 1)
        for d in range(1, S):
            bcopy(l, d).wait()

        def unpack(a, carry):
            act[pl.ds(a, NB, stride=128), :] = brecv[l, a].astype(jnp.float32)
            return carry
        lax.fori_loop(0, 128, unpack, 0, unroll=8)
        r = rbuf[l][0:1, :]

        def gate(b, total):
            value = pre[l, rows_of(b)]
            s = jax.nn.sigmoid(value)
            gp = (act[rows_of(b)] * s * (1.0 + value * (1.0 - s))).astype(jnp.bfloat16)
            gpbuf[rows_of(b)] = gp
            if last:
                return total
            w = jnp.dot(w1[l, b], gp, preferred_element_type=jnp.float32) * gcol[l, rows_of(b)]
            wbuf[rows_of(b)] = w
            u = z[l, rows_of(b)].astype(jnp.float32) * r
            return total + jnp.sum(w * u, axis=0, keepdims=True)
        total = lax.fori_loop(0, NB, gate, zero, unroll=UNROLL)
        if not last:
            sums_start(S + l, total)

        def grad_first(b, carry):
            u = z[l, rows_of(b)].astype(jnp.float32) * r
            normed = (u * gcol[l, rows_of(b)]).astype(jnp.bfloat16)
            gsend[l, 0, b // half, lax.rem(b, half)] = lax.dot_general(
                normed, gpbuf[rows_of(b)], NT, preferred_element_type=jnp.float32
            ).astype(jnp.bfloat16)
            return carry
        lax.fori_loop(0, NB, grad_first, 0, unroll=UNROLL)
        a_copy(l, 0).start()

        stage_b(l, 1)

        @pl.when(l < S - 1)
        def _():
            stage_c(l + 1, 1)

        @pl.when(l < S - 2)
        def _():
            stage_d(l + 2, 0)
        if last:
            return
        c = sums_wait(S + l) * (1.0 / D)

        def grad_in(b, carry):
            u = z[l, rows_of(b)].astype(jnp.float32) * r
            gf = gbuf[rows_of(b)].astype(jnp.float32) + r * (wbuf[rows_of(b)] - u * c)
            gbuf[rows_of(b)] = gf.astype(jnp.bfloat16)
            return carry
        lax.fori_loop(0, NB, grad_in, 0, unroll=UNROLL)

    def forward_step(l, carry):
        forward(l, False)
        return carry
    lax.fori_loop(0, S - 1, forward_step, 0)
    forward(S - 1, True)

    def backward_step(k, carry):
        l = S - 1 - k
        backward(l, False)
        back_send(l - 1)
        return carry
    lax.fori_loop(0, S - 1, backward_step, 0)
    backward(0, True)
    stage_d(1, 1)
    stage_b(0, 0)
    stage_c(1, 0)
    stage_c(0, 1)
    for l in range(S - 1, 1, -1):
        both(stage_e, l)
    stage_e(1, 1)
    stage_d(1, 0)
    stage_c(0, 0)
    stage_d(0, 1)
    stage_e(1, 0)
    stage_e(0, 1)
    stage_d(0, 0)
    stage_e(0, 0)
    for f in range(2):
        for d in range(NZ):
            e_copy(f, d).wait_recv()
    done = pltpu.make_async_copy(gath, out, osem.at[0])
    done.start()

    def finish(l, carry):
        for f in range(2):
            a_copy(l, f).wait_send()
            for d in range(1, NZ):
                b_copy(l, f, d).wait_send()

            @pl.when(me != l)
            def _():
                c_copy(l, f).wait_send()
        return carry
    lax.fori_loop(0, S, finish, 0)
    for f in range(2):
        for d in range(1, NZ):
            d_copy(f, d).wait_send()
        for d in range(NZ):
            e_copy(f, d).wait_send()
    done.wait()

    for d in range(1, S):
        weight_copy(0, d).wait_send()
    weight_copy(2, 1).wait_send()

    @pl.when(jnp.logical_not(even))
    def _():
        for d in range(2, S):
            weight_copy(2, d).wait_send()


UNROLL = 8


def local_step(S, NZ, NB, z0, cot, w1own, w2own, gown):
    F = NB * 128
    AC = 128 // S
    bf, f32 = jnp.bfloat16, jnp.float32
    vmem = pl.BlockSpec(memory_space=pltpu.VMEM)
    dma = pltpu.SemaphoreType.DMA
    half = NB // 2
    per = half // NZ
    shape = jax.ShapeDtypeStruct((2, S, 2, NZ, per, 128, 128), bf)
    return pl.pallas_call(
        functools.partial(step_kernel, S, NZ, NB),
        out_shape=shape,
        in_specs=[vmem] * 5,
        out_specs=pl.BlockSpec(memory_space=pl.ANY),
        scratch_shapes=[
            pltpu.VMEM((S, NB, 128, 128), bf),
            pltpu.VMEM((S, NB, 128, 128), bf),
            pltpu.VMEM((S, NB, 128), f32),
            pltpu.VMEM((S, F, 128), f32),
            pltpu.VMEM((S, F, 128), bf),
            pltpu.VMEM((S, F, 128), f32),
            pltpu.VMEM((F, 128), f32),
            pltpu.VMEM((S, 128, NB, 128), bf),
            pltpu.VMEM((S, S, AC, NB, 128), bf),
            pltpu.VMEM((S, S, AC, NB, 128), bf),
            pltpu.VMEM((S, 128, NB, 128), bf),
            pltpu.VMEM((F, 128), bf),
            pltpu.VMEM((F, 128), bf),
            pltpu.VMEM((F, 128), f32),
            pltpu.VMEM((2 * S, 8, 128), f32),
            pltpu.VMEM((2 * S, S - 1, 8, 128), f32),
            pltpu.VMEM((S, 8, 128), f32),
            pltpu.VMEM((S, 2, 2, half, 128, 128), bf),
            pltpu.VMEM((S, 2, half, 128, 128), bf),
            pltpu.VMEM((S, 2, half, 128, 128), bf),
            pltpu.VMEM((S, 2, NZ - 1, per, 128, 128), bf),
            pltpu.VMEM((S, 2, per, 128, 128), bf),
            pltpu.VMEM((2, S, 2, NZ, per, 128, 128), bf),
            dma((3, S - 1)),
            dma((3, S)),
            dma((S, S - 1)),
            dma((S, S - 1)),
            dma((S, S - 1)),
            dma((S, S - 1)),
            dma((2 * S, S - 1)),
            dma((2 * S, S - 1)),
            dma((S, 2)),
            dma((S, 2)),
            dma((S, 2, NZ - 1)),
            dma((S, 2, NZ - 1)),
            dma((S, 2)),
            dma((2, S)),
            dma((2, NZ - 1)),
            dma((2, NZ - 1)),
            dma((2, NZ)),
            dma((2, NZ)),
            dma((1,)),
        ],
        compiler_params=pltpu.CompilerParams(
            collective_id=0, has_side_effects=True, vmem_limit_bytes=58 * 1024 * 1024
        ),
        name="step",
    )(z0, cot, w1own, w2own, gown)


def fast_body(inputs, cotangent, first_factor, second_factor, gains, mixing, order):
    sections = lax.axis_size("section")
    first_block, second_block = first_factor[0], second_factor[0]
    blocks, size = first_block.shape[0], first_block.shape[1]
    NB = blocks // sections
    block_table, lane_table = mixing_tables(mixing[0], blocks, size)
    w1p = jnp.einsum(
        "bij,ja->bia", first_block, lane_table, preferred_element_type=jnp.float32
    ).astype(jnp.bfloat16)
    w2p = jnp.einsum(
        "be,qpej->qpbj", block_table, second_block.reshape(blocks, 2, blocks, size),
        preferred_element_type=jnp.float32,
    ).astype(jnp.bfloat16).reshape(blocks, size, size)
    rows = inputs.shape[0] * inputs.shape[1]
    z0 = jnp.take(inputs, order, axis=0).reshape(rows, -1).T
    cot = cotangent.reshape(rows, -1).T
    total = local_step(
        sections, lax.axis_size("dp") // 2, NB, z0, cot, w1p, w2p, gains[0].reshape(blocks, size)
    )
    t1 = total[0].reshape(blocks, size, size)
    t2 = total[1].reshape(blocks, 2, blocks, size)
    out1 = jnp.einsum(
        "bia,ja->bij", t1, lane_table, preferred_element_type=jnp.float32
    ).astype(jnp.bfloat16)
    out2 = jnp.einsum(
        "be,qpbj->qpej", block_table, t2, preferred_element_type=jnp.float32
    ).astype(jnp.bfloat16).reshape(blocks, size, size)
    return (out1[None], out2[None])


def solution(mesh):
    quick = mesh.shape["section"] == 4 and mesh.shape["dp"] == 8
    return jax.shard_map(
        fast_body if quick else body,
        mesh=mesh,
        in_specs=(
            P(None, "dp", "section"),
            P(None, "dp", "section"),
            P("section", None, None, None),
            P("section", None, None, None),
            P("section", None),
            P("section", None),
            P(),
        ),
        out_specs=(P("section", None, None, None), P("section", None, None, None)),
        check_vma=False,
    )
```
